32 devices in a mesh: dp: 8 (over z, x), tensor: 4 (over y, core).
Axes of the slice: x: 2, y: 2, z: 4, core: 2. Of those that a mesh axis runs over, the one named last changes fastest.
Arguments:
- tokens: bfloat16 [8192, 1024], P('dp'), may hold values from -6 to 6
- cotangent: bfloat16 [8192, 1024], P('dp'), may hold values from -6 to 6
- segments: int32 [8, 1024], P('dp'), may hold values from 0 to 3, never falling along the last dimension, each value on 1 to 512 neighbouring positions
- norm_gain: float32 [1024], replicated, may hold values from 0.5 to 1.5
- gate_proj: bfloat16 [1024, 2048], P(None, 'tensor'), may hold values from -0.1875 to 0.1875
- value_proj: bfloat16 [1024, 2048], P(None, 'tensor'), may hold values from -0.1875 to 0.1875
- shared_proj: bfloat16 [1024, 256], replicated, may hold values from -0.1875 to 0.1875
- step_proj: bfloat16 [1024, 32], P(None, 'tensor'), may hold values from -0.1875 to 0.1875
- conv_value: float32 [4, 2048], P(None, 'tensor'), may hold values from -3 to 3
- bias_value: float32 [2048], P('tensor'), may hold values from -3 to 3
- conv_shared: float32 [4, 256], replicated, may hold values from -3 to 3
- bias_shared: float32 [256], replicated, may hold values from -3 to 3
- step_bias: float32 [32], P('tensor'), may hold values from -3 to -1
- decay_log: float32 [32], P('tensor'), may hold values from -4 to 0.5
- skip_gain: float32 [32], P('tensor'), may hold values from 0.5 to 1.5
- gate_gain: float32 [2048], P('tensor'), may hold values from 0.5 to 1.5
- out_proj: bfloat16 [1024, 2048], P(None, 'tensor'), may hold values from -0.125 to 0.125
Outputs:
- result: bfloat16 [8192, 1024], P('dp')
- grad_tokens: bfloat16 [8192, 1024], P('dp')
- grad_norm_gain: float32 [1024], P('tensor')
- grad_gate_proj: float32 [1024, 2048], P('dp', 'tensor')
- grad_value_proj: float32 [1024, 2048], P('dp', 'tensor')
- grad_shared_proj: float32 [1024, 256], P('dp')
- grad_step_proj: float32 [1024, 32], P('dp', 'tensor')
- grad_conv_value: float32 [4, 2048], P(None, 'tensor')
- grad_bias_value: float32 [2048], P('tensor')
- grad_conv_shared: float32 [4, 256], replicated
- grad_bias_shared: float32 [256], replicated
- grad_step_bias: float32 [32], P('tensor')
- grad_decay_log: float32 [32], P('tensor')
- grad_skip_gain: float32 [32], P('tensor')
- grad_gate_gain: float32 [2048], P('tensor')
- grad_out_proj: float32 [1024, 2048], P('dp', 'tensor')
The draws below stay inside these ranges and needn't reach their ends.
Inputs may be any that keep to these rules, and one draw needn't show every extreme that they name: `segments`: within a row of 1024 tokens the numbers never fall; a segment holds 1 to 512 tokens.
All inputs are finite; a program needn't handle non-finite values.
Results may differ from the reference program's by a relative error of at most 0.012.
Values may be sent and summed in bfloat16 or wider, within the bound.
A program may use at most 192 MiB of HBM per device.

```python
import math
from functools import partial
import jax
import jax.numpy as jnp
import numpy as np
from jax import lax

D = 1024
H = 32
HSIZE = 64
N = 128
DI = 2048
CONV = 4
SPAN = 256
SEQ = 1024
ROWS = 8
TOKENS = 8192


def block_scale(rng, dims, cuts, smallest, largest):
    def one(position, shards_of):
        steps = jax.random.uniform(jax.random.fold_in(jax.random.fold_in(rng, 6), position), (shards_of,), jnp.float32, smallest / len(cuts), largest / len(cuts))
        return jnp.repeat(jnp.exp(steps), dims[position] // shards_of).reshape((-1,) + (1,) * (len(dims) - position - 1))

    level = one(*cuts[0])
    for cut in cuts[1:]:
        level = level * one(*cut)
    return level


def split_up(count, total, bound, lean):
    loads = [(1 << 20) // math.isqrt(rank ** lean) + 1 for rank in range(2, count + 1)]
    surplus, holding = total - bound - (count - 1), [1] * (count - 1)
    while surplus > 0:
        movable = [i for i in range(count - 1) if holding[i] < bound]
        mass, remaining = sum([loads[i] for i in movable]), surplus
        for i in movable:
            addition = min(bound - holding[i], max(1, remaining * loads[i] // mass), surplus)
            holding[i] = holding[i] + addition
            surplus = surplus - addition
    return np.array([bound] + holding)


def uneven_parts(own_key, amount, total, most, slope):
    if amount == 2:
        one = jax.random.randint(own_key, (), max(1, total - most), min(most, total - 1) + 1)
        return jnp.stack([one, total - one])
    lengths = jnp.asarray(split_up(amount, total, most, slope), jnp.int32)
    pairs = (amount - 1) // 2
    giver, taker = lengths[1:1 + 2 * pairs:2], lengths[2:2 + 2 * pairs:2]
    room = jnp.minimum(giver - 1, most - taker)
    passed = jax.random.randint(jax.random.fold_in(own_key, 1), (pairs,), 0, 1 << 20) % (room + 1)
    lengths = lengths.at[1:1 + 2 * pairs:2].set(giver - passed).at[2:2 + 2 * pairs:2].set(taker + passed)
    return lengths[jax.random.permutation(jax.random.fold_in(own_key, 2), amount)]


def bell_draw(stream_key, shape, spread, bound, cuts=(), held_as=jnp.bfloat16):
    loudness = block_scale(stream_key, shape, cuts, -0.22, 0.18) if cuts else 1.0
    values = jax.random.normal(stream_key, shape, jnp.float32) * spread * loudness
    return jnp.minimum(jnp.maximum(values, -bound), bound).astype(held_as)


def setup_inputs(seed: int = 0) -> dict:
    arg_keys = jax.random.split(jax.random.key(seed), 18)
    return {
        "tokens": bell_draw(arg_keys[0], (TOKENS, D), 1.0, 6.0, ((0, 8),)),
        "cotangent": bell_draw(arg_keys[1], (TOKENS, D), 1.0, 6.0, ((0, 8),)),
        "segments": jax.vmap(lambda own: jnp.searchsorted(jnp.cumsum(uneven_parts(own, 4, SEQ, SEQ // 2, 2)), jnp.arange(SEQ), side="right"))(jax.random.split(arg_keys[2], ROWS)).reshape((ROWS, SEQ)).astype(jnp.int32),
        "norm_gain": jnp.clip(1.0 + 0.1 * jax.random.normal(arg_keys[3], (D,), jnp.float32), 0.5, 1.5),
        "gate_proj": bell_draw(arg_keys[4], (D, DI), D ** -0.5, 0.1875, ((1, 4),)),
        "value_proj": bell_draw(arg_keys[5], (D, DI), D ** -0.5, 0.1875, ((1, 4),)),
        "shared_proj": bell_draw(arg_keys[6], (D, 2 * N), D ** -0.5, 0.1875),
        "step_proj": bell_draw(arg_keys[7], (D, H), D ** -0.5, 0.1875, ((1, 4),)),
        "conv_value": bell_draw(arg_keys[8], (CONV, DI), CONV ** -0.5, 3.0, ((1, 4),), jnp.float32),
        "bias_value": bell_draw(arg_keys[9], (DI,), 0.5, 3.0, ((0, 4),), jnp.float32),
        "conv_shared": bell_draw(arg_keys[10], (CONV, 2 * N), CONV ** -0.5, 3.0, (), jnp.float32),
        "bias_shared": bell_draw(arg_keys[11], (2 * N,), 0.5, 3.0, (), jnp.float32),
        "step_bias": jnp.clip(-3.0 + 2.0 * jax.random.uniform(arg_keys[12], (H,), jnp.float32) ** block_scale(arg_keys[12], (H,), ((0, 4),), -0.2, 0.2), -3.0, -1.0),
        "decay_log": jnp.clip(-4.0 + 4.5 * jax.random.uniform(arg_keys[13], (H,), jnp.float32) ** block_scale(arg_keys[13], (H,), ((0, 4),), -0.2, 0.2), -4.0, 0.5),
        "skip_gain": jnp.clip(0.5 + 1.0 * jax.random.uniform(arg_keys[14], (H,), jnp.float32) ** block_scale(arg_keys[14], (H,), ((0, 4),), -0.2, 0.2), 0.5, 1.5),
        "gate_gain": jnp.clip(1.0 + 0.1 * jax.random.normal(arg_keys[15], (DI,), jnp.float32), 0.5, 1.5),
        "out_proj": bell_draw(arg_keys[16], (D, DI), DI ** -0.5, 0.125, ((1, 4),)),
    }


EPSILON = 1e-05
NEG_FILL = -1e+30
EXACT = lax.Precision.HIGHEST

def silu_grad(inputs):
    sigmoid = jax.nn.sigmoid(inputs)
    return sigmoid * (1.0 + inputs * (1.0 - sigmoid))

def causal_conv(inputs, kernel, shift_bias, seg_ids):
    kernel_len = kernel.shape[0]
    length = inputs.shape[0]
    padded = jnp.pad(inputs, ((kernel_len - 1, 0), (0, 0)))
    padded_ids = jnp.pad(seg_ids, (kernel_len - 1, 0), constant_values=-1)
    result = jnp.zeros_like(inputs) + shift_bias[None, :]
    for offset in range(kernel_len):
        shifted = padded[offset:offset + length]
        same_doc = (padded_ids[offset:offset + length] == seg_ids)[:, None]
        result = result + jnp.where(same_doc, shifted, 0.0) * kernel[offset][None, :]
    return result

def state_scan(values, step_sizes, decay_rates, write_in, read_out, seg_ids):
    length, head_count, head_size = values.shape
    state_size = write_in.shape[1]
    blocks = length // SPAN

    def one_block(carried, pieces):
        memory, last_id = carried
        block_vals, block_steps, block_write, block_read, block_ids = pieces
        log_decay = jnp.cumsum(block_steps * decay_rates[None, :], axis=0)
        intersections = jnp.dot(block_read, block_write.T, precision=EXACT, preferred_element_type=jnp.float32)
        causal = jnp.arange(SPAN)[:, None] >= jnp.arange(SPAN)[None, :]
        allowed = causal & (block_ids[:, None] == block_ids[None, :])
        gaps = log_decay[:, None, :] - log_decay[None, :, :]
        weights = jnp.exp(jnp.where(allowed[:, :, None], gaps, NEG_FILL)) * intersections[:, :, None]
        scaled = block_vals * block_steps[:, :, None]
        within = jnp.einsum('tsh,shp->thp', weights, scaled, precision=EXACT)
        entering = (block_ids == last_id).astype(jnp.float32)
        carried_in = jnp.einsum('tn,hnp->thp', block_read, memory, precision=EXACT)
        carried_in = carried_in * (jnp.exp(log_decay) * entering[:, None])[:, :, None]
        leaving = (block_ids == block_ids[-1]).astype(jnp.float32)
        to_end = jnp.exp(log_decay[-1][None, :] - log_decay) * leaving[:, None]
        fresh = jnp.einsum('sn,shp->hnp', block_write, scaled * to_end[:, :, None], precision=EXACT)
        continued = (block_ids[-1] == last_id).astype(jnp.float32)
        memory = memory * (continued * jnp.exp(log_decay[-1]))[:, None, None] + fresh
        return ((memory, block_ids[-1]), within + carried_in)
    pieces = (values.reshape(blocks, SPAN, head_count, head_size), step_sizes.reshape(blocks, SPAN, head_count), write_in.reshape(blocks, SPAN, state_size), read_out.reshape(blocks, SPAN, state_size), seg_ids.reshape(blocks, SPAN))
    initial = (jnp.zeros((head_count, state_size, head_size), values.dtype), jnp.array(-1, seg_ids.dtype))
    final_state, outputs = lax.scan(one_block, initial, pieces)
    return outputs.reshape(length, head_count, head_size)

def value_path(value_pre, step_pre, conv_value, bias_value, step_bias, decay_log, skip_gain, write_in, read_out, seg_ids):
    activated = jax.nn.silu(causal_conv(value_pre, conv_value, bias_value, seg_ids))
    step_sizes = jax.nn.softplus(step_pre + step_bias[None, :])
    decay_rates = -jnp.exp(decay_log)
    length = activated.shape[0]
    head_count = step_pre.shape[1]
    values = activated.reshape(length, head_count, HSIZE)
    mixed = state_scan(values, step_sizes, decay_rates, write_in, read_out, seg_ids) + values * skip_gain[None, :, None]
    return mixed.reshape(length, head_count * HSIZE)

def shared_path(shared_pre, conv_shared, bias_shared, seg_ids):
    activated = jax.nn.silu(causal_conv(shared_pre, conv_shared, bias_shared, seg_ids))
    half_width = activated.shape[1] // 2
    return (activated[:, :half_width], activated[:, half_width:])

def back_dot(left, right):
    return lax.dot_general(left, right, (((1,), (1,)), ((), ())), preferred_element_type=jnp.float32)

def left_dot(left, right):
    return lax.dot_general(left, right, (((0,), (0,)), ((), ())), preferred_element_type=jnp.float32)

def reference(tokens, cotangent, segments, norm_gain, gate_proj, value_proj, shared_proj, step_proj, conv_value, bias_value, conv_shared, bias_shared, step_bias, decay_log, skip_gain, gate_gain, out_proj):
    row_count = segments.shape[0]
    row_len = segments.shape[1]
    token_rows = tokens.reshape(row_count, row_len, D)
    cot_rows = cotangent.reshape(row_count, row_len, D)

    def row_pass(totals, row_data):
        row_tokens, row_cot, seg_ids = row_data
        inputs_f = row_tokens.astype(jnp.float32)
        inv_in = lax.rsqrt(lax.optimization_barrier(jnp.mean(inputs_f * inputs_f, axis=1, keepdims=True)) + EPSILON)
        normed = inputs_f * inv_in
        hidden = (normed * norm_gain[None, :]).astype(jnp.bfloat16)
        gate_pre = jnp.dot(hidden, gate_proj, preferred_element_type=jnp.float32)
        value_pre = jnp.dot(hidden, value_proj, preferred_element_type=jnp.float32)
        shared_pre = jnp.dot(hidden, shared_proj, preferred_element_type=jnp.float32)
        step_pre = jnp.dot(hidden, step_proj, preferred_element_type=jnp.float32)
        (write_in, read_out), shared_back = jax.vjp(partial(shared_path, seg_ids=seg_ids), shared_pre, conv_shared, bias_shared)
        mixer, mixer_back = jax.vjp(partial(value_path, seg_ids=seg_ids), value_pre, step_pre, conv_value, bias_value, step_bias, decay_log, skip_gain, write_in, read_out)
        gate_act = jax.nn.silu(gate_pre)
        gated = mixer * gate_act
        inv_gate = lax.rsqrt(lax.optimization_barrier(jnp.sum(gated * gated, axis=1)) / DI + EPSILON)[:, None]
        normal_out = (gated * inv_gate * gate_gain[None, :]).astype(jnp.bfloat16)
        mixed = back_dot(normal_out, out_proj)
        row_result = (inputs_f + mixed).astype(jnp.bfloat16)
        upstream = row_cot.astype(jnp.float32)
        grad_normal = jnp.dot(row_cot, out_proj, preferred_element_type=jnp.float32)
        grad_gate_gain = lax.optimization_barrier(jnp.sum(grad_normal * gated * inv_gate, axis=0))
        weighted = grad_normal * gate_gain[None, :]
        dots_gate = lax.optimization_barrier(jnp.sum(weighted * gated, axis=1))
        grad_gated = inv_gate * weighted - gated * (inv_gate * inv_gate * inv_gate) * (dots_gate / DI)[:, None]
        grad_mixer = grad_gated * gate_act
        grad_gate_pre = grad_gated * mixer * silu_grad(gate_pre)
        grad_value_pre, grad_step_pre, grad_conv_value, grad_bias_value, grad_step_bias, grad_decay_log, grad_skip_gain, write_grad, read_grad = mixer_back(grad_mixer)
        grad_shared_pre, grad_conv_shared, grad_bias_shared = shared_back((write_grad, read_grad))
        gate_low = grad_gate_pre.astype(jnp.bfloat16)
        value_low = grad_value_pre.astype(jnp.bfloat16)
        step_low = grad_step_pre.astype(jnp.bfloat16)
        shared_low = grad_shared_pre.astype(jnp.bfloat16)
        grad_hidden = back_dot(gate_low, gate_proj) + back_dot(value_low, value_proj) + back_dot(step_low, step_proj)
        grad_hidden = grad_hidden + back_dot(shared_low, shared_proj)
        grad_norm_gain = lax.optimization_barrier(jnp.sum(grad_hidden * normed, axis=0))
        scaled = grad_hidden * norm_gain[None, :]
        grad_row = inv_in * (scaled - normed * lax.optimization_barrier(jnp.mean(scaled * normed, axis=1, keepdims=True))) + upstream
        grad_row = grad_row.astype(jnp.bfloat16)
        terms = (grad_norm_gain, left_dot(hidden, gate_low), left_dot(hidden, value_low), left_dot(hidden, shared_low), left_dot(hidden, step_low), grad_conv_value, grad_bias_value, grad_conv_shared, grad_bias_shared, grad_step_bias, grad_decay_log, grad_skip_gain, grad_gate_gain, left_dot(row_cot, normal_out))
        totals = tuple((total + term for total, term in zip(totals, terms)))
        return (totals, (row_result, grad_row))
    params = (norm_gain, gate_proj, value_proj, shared_proj, step_proj, conv_value, bias_value, conv_shared, bias_shared, step_bias, decay_log, skip_gain, gate_gain, out_proj)
    initial = tuple((jnp.zeros(param.shape, jnp.float32) for param in params))
    finals, (result_rows, grad_rows) = lax.scan(row_pass, initial, (token_rows, cot_rows, segments))
    return (result_rows.reshape(tokens.shape), grad_rows.reshape(tokens.shape), finals[0], finals[1], finals[2], finals[3], finals[4], finals[5], finals[6], finals[7], finals[8], finals[9], finals[10], finals[11], finals[12], finals[13])
```

```python
import jax
import jax.numpy as jnp
from jax import lax
from jax.experimental import pallas as pl
from jax.experimental.pallas import tpu as pltpu
from jax.sharding import PartitionSpec as P

SPAN = 256
HSIZE = 64
LANES = 128
EPSILON = 1e-05
NEG_FILL = -1e30
EXACT = lax.Precision.HIGHEST
F32 = jnp.float32
BF16 = jnp.bfloat16


def mm(left, right):
    return jnp.dot(left, right, preferred_element_type=F32)


def mm_t(left, right):
    return lax.dot_general(left, right, (((1,), (1,)), ((), ())), preferred_element_type=F32)


def t_mm(left, right):
    return lax.dot_general(left, right, (((0,), (0,)), ((), ())), preferred_element_type=F32)


def exact(left, right):
    return jnp.dot(left, right, precision=EXACT, preferred_element_type=F32)


def sigmoid(v):
    return 1.0 / (1.0 + jnp.exp(-v))


def spread(cols, pairs):
    low = lax.broadcasted_iota(jnp.int32, (cols.shape[0], LANES), 1) < HSIZE
    parts = [
        jnp.where(low, cols[:, 2 * p : 2 * p + 1], cols[:, 2 * p + 1 : 2 * p + 2])
        for p in range(pairs)
    ]
    return jnp.concatenate(parts, axis=1)


def gather_mat(inner):
    channel = lax.broadcasted_iota(jnp.int32, (inner, LANES), 0) // HSIZE
    head = lax.broadcasted_iota(jnp.int32, (inner, LANES), 1)
    return (channel == head).astype(F32)


def grid_masks():
    row = lax.broadcasted_iota(jnp.int32, (SPAN, SPAN), 0)
    col = lax.broadcasted_iota(jnp.int32, (SPAN, SPAN), 1)
    return row, col


def conv_fwd(buf, pack, aux):
    out = pack[4:5, :] + buf[8 : 8 + SPAN, :] * pack[3:4, :]
    for j in range(1, 4):
        out = out + buf[8 - j : 8 - j + SPAN, :] * (aux[:, j : j + 1] * pack[3 - j : 4 - j, :])
    return out


def fwd_kernel(
    tok, cot, aux_ref, segr, ng, wg, wv, ws, wst, wo, chp, shp, hp,
    hidden_o, gate_o, vpre_o, cv_o, spre_o, scv_o, z_o, ld_o, ldt_o, yn_o, sin_o, gn_o, stat_o,
    vbuf, sbuf, state,
):
    inner = wg.shape[1]
    pairs = inner // LANES
    state_size = ws.shape[1] // 2

    @pl.when(pl.program_id(0) == 0)
    def _():
        vbuf[0:8, :] = jnp.zeros((8, inner), F32)
        sbuf[0:8, :] = jnp.zeros((8, 2 * state_size), F32)
        state[...] = jnp.zeros_like(state)

    aux = aux_ref[...]
    x = tok[...].astype(F32)
    inv = lax.rsqrt(jnp.mean(x * x, axis=1, keepdims=True) + EPSILON)
    hid = (x * inv * ng[...]).astype(BF16)
    hidden_o[...] = hid
    gate = mm(hid, wg[...])
    gate_o[...] = gate
    vp = mm(hid, wv[...])
    vpre_o[...] = vp
    vbuf[8 : 8 + SPAN, :] = vp
    sp = mm(hid, ws[...])
    spre_o[...] = sp
    sbuf[8 : 8 + SPAN, :] = sp
    z = mm(hid, wst[...]) + hp[0:1, :]
    z_o[...] = z
    gn = mm(cot[...], wo[...])
    gn_o[...] = gn
    scv = conv_fwd(sbuf, shp, aux)
    scv_o[...] = scv
    bc = (scv * sigmoid(scv)).astype(BF16)
    b_low, c_low = bc[:, :state_size], bc[:, state_size:]
    cv = conv_fwd(vbuf, chp, aux)
    cv_o[...] = cv
    vbuf[0:8, :] = vbuf[SPAN : SPAN + 8, :]
    sbuf[0:8, :] = sbuf[SPAN : SPAN + 8, :]
    values = cv * sigmoid(cv)
    dt = jnp.maximum(z, 0.0) + jnp.log1p(jnp.exp(-jnp.abs(z)))
    row, col = grid_masks()
    tri = (row >= col).astype(F32)
    ld = exact(tri, dt * hp[1:2, :])
    ld_o[...] = ld
    ldt = jnp.transpose(ld)[0:8, :]
    ldt_o[...] = ldt
    allowed = (row >= col) & (aux[:, 0:1] == segr[...])
    scores = jnp.where(allowed, mm_t(c_low, b_low), 0.0)
    xs = values * spread(dt, pairs)
    xs_low = xs.astype(BF16)
    ein = jnp.exp(ld) * aux[:, 4:5]
    eout = jnp.exp(ld[SPAN - 1 : SPAN, :] - ld) * aux[:, 5:6]
    ein_x = spread(ein, pairs)
    eout_x = spread(eout, pairs)
    old = state[...]
    sin_o[...] = old
    carried = mm(c_low, old.astype(BF16)) * ein_x
    state[...] = old * ein_x[SPAN - 1 : SPAN, :] + t_mm(b_low, (xs * eout_x).astype(BF16))
    low = lax.broadcasted_iota(jnp.int32, (SPAN, LANES), 1) < HSIZE
    parts = []
    for p in range(pairs):
        pair = xs_low[:, p * LANES : (p + 1) * LANES]
        outs = []
        for h in (2 * p, 2 * p + 1):
            gap = jnp.minimum(ld[:, h : h + 1] - ldt[h : h + 1, :], 0.0)
            outs.append(mm((jnp.exp(gap) * scores).astype(BF16), pair))
        parts.append(jnp.where(low, outs[0], outs[1]))
    yn = jnp.concatenate(parts, axis=1) + carried
    yn_o[...] = yn
    gated = (yn + chp[6:7, :] * values) * (gate * sigmoid(gate))
    squares = jnp.sum(gated * gated, axis=1, keepdims=True)
    dots = jnp.sum(gn * chp[5:6, :] * gated, axis=1, keepdims=True)
    lane = lax.broadcasted_iota(jnp.int32, (SPAN, LANES), 1)
    both = jnp.where(lane == 0, squares, jnp.where(lane == 1, dots, 0.0))
    stat_o[...] = jnp.transpose(both)[0:8, :]


def gate_kernel(
    width, gate_ref, cv_ref, yn, gn_ref, stat, chp, wo, normal_o, dy_o, low_o, gain_o, mixed_o
):
    both = jnp.transpose(jnp.concatenate([stat[...]] * (LANES // 8), axis=0))
    inv = lax.rsqrt(both[:, 0:1] / width + EPSILON)
    mean_dots = both[:, 1:2] / width
    gate = gate_ref[...]
    cv = cv_ref[...]
    gn = gn_ref[...]
    sig = sigmoid(gate)
    act = gate * sig
    mixer = yn[...] + chp[6:7, :] * (cv * sigmoid(cv))
    gated = mixer * act
    normed = gated * inv
    normal = (normed * chp[5:6, :]).astype(BF16)
    normal_o[...] = normal
    mixed_o[...] = mm_t(normal, wo[...]).astype(BF16)
    part = jnp.sum(gn * normed, axis=0, keepdims=True)

    @pl.when(pl.program_id(0) == 0)
    def _():
        gain_o[...] = jnp.zeros_like(gain_o)

    gain_o[0:1, :] += part
    grad_gated = inv * (gn * chp[5:6, :]) - gated * (inv * inv * inv) * mean_dots
    dy_o[...] = grad_gated * act
    low_o[...] = (grad_gated * mixer * (sig * (1.0 + gate * (1.0 - sig)))).astype(BF16)


def bwd_kernel(
    dy_ref, cv_ref, vpre, scv_ref, z_ref, ld_ref, ldt_ref, yn, sin, aux_ref, segr, glow,
    wg, wv, wst, chp, hp,
    vlow_o, slow_o, dbc_o, heads_o, chg_o, hg_o,
    dbuf, dstate,
):
    inner = wg.shape[1]
    pairs = inner // LANES
    state_size = sin.shape[0]

    @pl.when(pl.program_id(0) == 0)
    def _():
        dbuf[SPAN : SPAN + 8, :] = jnp.zeros((8, inner), F32)
        dstate[...] = jnp.zeros_like(dstate)
        chg_o[...] = jnp.zeros_like(chg_o)
        hg_o[...] = jnp.zeros_like(hg_o)

    aux = aux_ref[...]
    dy = dy_ref[...]
    dy_low = dy.astype(BF16)
    scv = scv_ref[...]
    bc = (scv * sigmoid(scv)).astype(BF16)
    b_low, c_low = bc[:, :state_size], bc[:, state_size:]
    cv = cv_ref[...]
    csig = sigmoid(cv)
    values = cv * csig
    z = z_ref[...]
    dt = jnp.maximum(z, 0.0) + jnp.log1p(jnp.exp(-jnp.abs(z)))
    ld = ld_ref[...]
    ldt = ldt_ref[...]
    dt_x = spread(dt, pairs)
    xs = values * dt_x
    xs_low = xs.astype(BF16)
    ein = jnp.exp(ld) * aux[:, 4:5]
    eout = jnp.exp(ld[SPAN - 1 : SPAN, :] - ld) * aux[:, 5:6]
    ein_x = spread(ein, pairs)
    eout_x = spread(eout, pairs)
    row, col = grid_masks()
    allowed = (col >= row) & (aux[:, 0:1] == segr[...])
    mask = allowed.astype(F32)
    scores_t = mm_t(b_low, c_low) * mask
    low = lax.broadcasted_iota(jnp.int32, (SPAN, LANES), 1) < HSIZE
    parts = []
    dscores_t = jnp.zeros((SPAN, SPAN), F32)
    for p in range(pairs):
        cols = slice(p * LANES, (p + 1) * LANES)
        dy_pair = dy_low[:, cols]
        xs_pair = xs_low[:, cols]
        zero = jnp.zeros_like(xs_pair)
        outs = []
        for side, h in enumerate((2 * p, 2 * p + 1)):
            gap = jnp.minimum(ldt[h : h + 1, :] - ld[:, h : h + 1], 0.0)
            decay = jnp.exp(gap)
            outs.append(mm((decay * scores_t).astype(BF16), dy_pair))
            mine = jnp.where(low, xs_pair, zero) if side == 0 else jnp.where(low, zero, xs_pair)
            dscores_t = dscores_t + mm_t(mine, dy_pair) * decay
        parts.append(jnp.where(low, outs[0], outs[1]))
    inside = jnp.concatenate(parts, axis=1)
    dscores_low = (dscores_t * mask).astype(BF16)
    old = sin[...]
    dst = dstate[...]
    dst_low = dst.astype(BF16)
    dye_low = (dy * ein_x).astype(BF16)
    xse_low = (xs * eout_x).astype(BF16)
    db = mm(dscores_low, c_low) + mm_t(xse_low, dst_low)
    dc = t_mm(dscores_low, b_low) + mm_t(dye_low, old.astype(BF16))
    dbc_o[...] = jnp.concatenate([db, dc], axis=1)
    late = mm(b_low, dst_low) * eout_x
    keep = ein_x[SPAN - 1 : SPAN, :]
    dstate[...] = dst * keep + t_mm(c_low, dye_low)
    dxs = inside + late
    collect = gather_mat(inner)
    q = dy_low.astype(F32) * yn[...] - xs_low.astype(F32) * inside
    u = xs * late
    kappa = exact(jnp.sum(old * dst, axis=0, keepdims=True) * keep + jnp.zeros((8, inner), F32), collect)
    da = (
        exact((col >= row).astype(F32), exact(q, collect))
        + exact((row > col).astype(F32), exact(u, collect))
        + kappa[0:1, :]
    )
    rates = hp[1:2, :]
    ddt = da * rates + exact(dxs * values, collect)
    dz = ddt * sigmoid(z)
    slow = dz.astype(BF16)
    slow_o[...] = slow
    skip = exact(jnp.sum(dy * values, axis=0, keepdims=True) + jnp.zeros((8, inner), F32), collect)
    hg_o[0:1, :] += jnp.sum(dz, axis=0, keepdims=True)
    hg_o[1:2, :] += jnp.sum(da * dt, axis=0, keepdims=True) * rates
    hg_o[2:3, :] += skip[0:1, :]
    dcv = (dxs * dt_x + chp[6:7, :] * dy) * (csig * (1.0 + cv * (1.0 - csig)))
    dbuf[0:SPAN, :] = dcv
    vp = vpre[...]
    dv = dcv * chp[3:4, :]
    chg_o[3:4, :] += jnp.sum(dcv * vp, axis=0, keepdims=True)
    chg_o[4:5, :] += jnp.sum(dcv, axis=0, keepdims=True)
    for j in range(1, 4):
        moved = dbuf[j : j + SPAN, :] * aux[:, 8 + j : 9 + j]
        dv = dv + moved * chp[3 - j : 4 - j, :]
        chg_o[3 - j : 4 - j, :] += jnp.sum(moved * vp, axis=0, keepdims=True)
    dbuf[SPAN : SPAN + 8, :] = dbuf[0:8, :]
    vlow = dv.astype(BF16)
    vlow_o[...] = vlow
    heads_o[...] = (
        mm_t(glow[...], wg[...]) + mm_t(vlow, wv[...]) + mm_t(slow, wst[...])
    ).astype(BF16)


def end_kernel(
    dbc, scv_ref, spre, aux_ref, heads, tok, cot, mixed, ng, ws, shp,
    result_o, gtok_o, shlow_o, shg_o, norm_o,
    dbuf,
):
    width = ws.shape[1]

    @pl.when(pl.program_id(0) == 0)
    def _():
        dbuf[SPAN : SPAN + 8, :] = jnp.zeros((8, width), F32)
        shg_o[...] = jnp.zeros_like(shg_o)
        norm_o[...] = jnp.zeros_like(norm_o)

    aux = aux_ref[...]
    scv = scv_ref[...]
    csig = sigmoid(scv)
    dcv = dbc[...] * (csig * (1.0 + scv * (1.0 - csig)))
    dbuf[0:SPAN, :] = dcv
    sp = spre[...]
    ds = dcv * shp[3:4, :]
    shg_o[3:4, :] += jnp.sum(dcv * sp, axis=0, keepdims=True)
    shg_o[4:5, :] += jnp.sum(dcv, axis=0, keepdims=True)
    for j in range(1, 4):
        moved = dbuf[j : j + SPAN, :] * aux[:, 8 + j : 9 + j]
        ds = ds + moved * shp[3 - j : 4 - j, :]
        shg_o[3 - j : 4 - j, :] += jnp.sum(moved * sp, axis=0, keepdims=True)
    dbuf[SPAN : SPAN + 8, :] = dbuf[0:8, :]
    shlow = ds.astype(BF16)
    shlow_o[...] = shlow
    grad_hidden = heads[...].astype(F32) + mm_t(shlow, ws[...])
    x = tok[...].astype(F32)
    inv = lax.rsqrt(jnp.mean(x * x, axis=1, keepdims=True) + EPSILON)
    normed = x * inv
    scaled = grad_hidden * ng[...]
    norm_o[0:1, :] += jnp.sum(grad_hidden * normed, axis=0, keepdims=True)
    mean = jnp.mean(scaled * normed, axis=1, keepdims=True)
    gtok_o[...] = (inv * (scaled - normed * mean) + cot[...].astype(F32)).astype(BF16)
    result_o[...] = (x + mixed[...].astype(F32)).astype(BF16)


def call(body, blocks, ins, outs, scratch, backward, name):
    def spec(shape, kind):
        if kind == "whole":
            return pl.BlockSpec(shape, lambda i: (0,) * len(shape))
        if kind == "lanes":
            block = (shape[0], shape[1] // blocks)
            return pl.BlockSpec(block, (lambda i: (0, blocks - 1 - i)) if backward else (lambda i: (0, i)))
        block = (shape[0] // blocks, shape[1])
        return pl.BlockSpec(block, (lambda i: (blocks - 1 - i, 0)) if backward else (lambda i: (i, 0)))

    return pl.pallas_call(
        body,
        grid=(blocks,),
        in_specs=[spec(a.shape, kind) for a, kind in ins],
        out_specs=[spec(shape, kind) for shape, _, kind in outs],
        out_shape=[jax.ShapeDtypeStruct(shape, dtype) for shape, dtype, _ in outs],
        scratch_shapes=scratch,
        compiler_params=pltpu.CompilerParams(
            dimension_semantics=("arbitrary",), vmem_limit_bytes=60 * 1024 * 1024
        ),
        name=name,
    )(*[a for a, _ in ins])


def pad_rows(parts, width):
    rows = [jnp.pad(p.astype(F32), ((0, 0), (0, width - p.shape[1]))) for p in parts]
    used = sum(r.shape[0] for r in rows)
    return jnp.concatenate(rows + [jnp.zeros((8 - used, width), F32)], axis=0)


def per_device(
    tokens, cotangent, segments, norm_gain, gate_proj, value_proj, shared_proj, step_proj,
    conv_value, bias_value, conv_shared, bias_shared, step_bias, decay_log, skip_gain,
    gate_gain, out_proj,
):
    tp_count = lax.axis_size("tensor")
    length, width = tokens.shape
    inner = gate_proj.shape[1]
    heads = step_proj.shape[1]
    shared_width = shared_proj.shape[1]
    state_size = shared_width // 2
    blocks = length // SPAN
    ids = segments[0]
    back = [jnp.concatenate([jnp.full((j,), -1, ids.dtype), ids[: length - j]]) for j in range(4)]
    ahead = [jnp.concatenate([ids[j:], jnp.full((j,), -1, ids.dtype)]) for j in range(4)]
    ends = ids.reshape(blocks, SPAN)[:, -1]
    before = jnp.concatenate([jnp.full((1,), -1, ids.dtype), ends[:-1]])
    entering = ids == jnp.repeat(before, SPAN)
    leaving = ids == jnp.repeat(ends, SPAN)
    columns = (
        [ids] + [b == ids for b in back[1:]] + [entering, leaving, ids, ids, ids]
        + [a == ids for a in ahead[1:]]
    )
    aux = jnp.stack([c.astype(F32) for c in columns], axis=1)
    segr = ids.astype(F32)[None, :]
    ng = norm_gain[None, :]
    wst = jnp.pad(step_proj, ((0, 0), (0, LANES - heads)))
    chp = pad_rows(
        [conv_value, bias_value[None], gate_gain[None], jnp.repeat(skip_gain, HSIZE)[None]], inner
    )
    shp = pad_rows([conv_shared, bias_shared[None]], shared_width)
    hp = pad_rows([step_bias[None], -jnp.exp(decay_log)[None]], LANES)

    (
        hidden, gate_pre, value_pre, conv_out, shared_pre, shared_conv, z, ld, ldt, yn, sin, gn, stat,
    ) = call(
        fwd_kernel,
        blocks,
        [
            (tokens, "rows"), (cotangent, "rows"), (aux, "rows"), (segr, "lanes"), (ng, "whole"),
            (gate_proj, "whole"), (value_proj, "whole"), (shared_proj, "whole"), (wst, "whole"),
            (out_proj, "whole"), (chp, "whole"), (shp, "whole"), (hp, "whole"),
        ],
        [
            ((length, width), BF16, "rows"),
            ((length, inner), F32, "rows"),
            ((length, inner), F32, "rows"),
            ((length, inner), F32, "rows"),
            ((length, shared_width), F32, "rows"),
            ((length, shared_width), F32, "rows"),
            ((length, LANES), F32, "rows"),
            ((length, LANES), F32, "rows"),
            ((8, length), F32, "lanes"),
            ((length, inner), F32, "rows"),
            ((blocks * state_size, inner), F32, "rows"),
            ((length, inner), F32, "rows"),
            ((8, length), F32, "lanes"),
        ],
        [
            pltpu.VMEM((SPAN + 8, inner), F32),
            pltpu.VMEM((SPAN + 8, shared_width), F32),
            pltpu.VMEM((state_size, inner), F32),
        ],
        False,
        "fwd_scan",
    )
    stat = lax.psum(stat, "tensor")
    total_inner = float(inner * tp_count)

    def gate_body(*refs):
        gate_kernel(total_inner, *refs)

    normal_out, dy, gate_low, gain_part, mixed_part = call(
        gate_body,
        blocks,
        [
            (gate_pre, "rows"), (conv_out, "rows"), (yn, "rows"), (gn, "rows"), (stat, "lanes"),
            (chp, "whole"), (out_proj, "whole"),
        ],
        [
            ((length, inner), BF16, "rows"),
            ((length, inner), F32, "rows"),
            ((length, inner), BF16, "rows"),
            ((8, inner), F32, "whole"),
            ((length, width), BF16, "rows"),
        ],
        [],
        False,
        "gate_step",
    )
    mixed = lax.psum(mixed_part, "tensor")
    early = lax.psum_scatter(
        jnp.concatenate([t_mm(hidden, gate_low), t_mm(cotangent, normal_out)], axis=1).astype(BF16),
        "dp",
        scatter_dimension=0,
        tiled=True,
    ).astype(F32)
    value_low, step_low, dbc, heads_part, ch_grads, head_grads = call(
        bwd_kernel,
        blocks,
        [
            (dy, "rows"), (conv_out, "rows"), (value_pre, "rows"), (shared_conv, "rows"),
            (z, "rows"), (ld, "rows"), (ldt, "lanes"), (yn, "rows"), (sin, "rows"),
            (aux, "rows"), (segr, "lanes"), (gate_low, "rows"), (gate_proj, "whole"),
            (value_proj, "whole"), (wst, "whole"), (chp, "whole"), (hp, "whole"),
        ],
        [
            ((length, inner), BF16, "rows"),
            ((length, LANES), BF16, "rows"),
            ((length, shared_width), F32, "rows"),
            ((length, width), BF16, "rows"),
            ((8, inner), F32, "whole"),
            ((8, LANES), F32, "whole"),
        ],
        [pltpu.VMEM((SPAN + 8, inner), F32), pltpu.VMEM((state_size, inner), F32)],
        True,
        "bwd_scan",
    )
    dbc = lax.psum(dbc, "tensor")
    heads_sum = lax.psum(heads_part, "tensor")
    result, grad_tokens, shared_low, sh_grads, norm_part = call(
        end_kernel,
        blocks,
        [
            (dbc, "rows"), (shared_conv, "rows"), (shared_pre, "rows"), (aux, "rows"),
            (heads_sum, "rows"), (tokens, "rows"), (cotangent, "rows"), (mixed, "rows"),
            (ng, "whole"), (shared_proj, "whole"), (shp, "whole"),
        ],
        [
            ((length, width), BF16, "rows"),
            ((length, width), BF16, "rows"),
            ((length, shared_width), BF16, "rows"),
            ((8, shared_width), F32, "whole"),
            ((8, width), F32, "whole"),
        ],
        [pltpu.VMEM((SPAN + 8, shared_width), F32)],
        True,
        "end_step",
    )
    late = lax.psum_scatter(
        t_mm(hidden, jnp.concatenate([value_low, shared_low, step_low], axis=1)).astype(BF16),
        "dp",
        scatter_dimension=0,
        tiled=True,
    ).astype(F32)
    col_width = width // tp_count
    norm_mine = lax.dynamic_slice_in_dim(
        norm_part[0], lax.axis_index("tensor") * col_width, col_width, 0
    )
    packed = jnp.concatenate(
        [
            norm_mine, ch_grads[:5].reshape(-1), sh_grads[:5].reshape(-1),
            head_grads[:3].reshape(-1), gain_part[0],
        ]
    )
    packed = lax.psum(packed.reshape(-1, LANES), "dp").reshape(-1)
    sizes = [col_width, 5 * inner, 5 * shared_width, 3 * LANES, inner]
    pieces, start = [], 0
    for size in sizes:
        pieces.append(packed[start : start + size])
        start += size
    channel = pieces[1].reshape(5, inner)
    shared = pieces[2].reshape(5, shared_width)
    per_head = pieces[3].reshape(3, LANES)[:, :heads]
    return (
        result,
        grad_tokens,
        pieces[0],
        early[:, :inner],
        late[:, :inner],
        late[:, inner : inner + shared_width],
        late[:, inner + shared_width : inner + shared_width + heads],
        channel[:4],
        channel[4],
        shared[:4],
        shared[4],
        per_head[0],
        per_head[1],
        per_head[2],
        pieces[4],
        early[:, inner:],
    )


def solution(mesh):
    rows, cols, vec = P("dp", None), P(None, "tensor"), P("tensor")
    return jax.shard_map(
        per_device,
        mesh=mesh,
        in_specs=(
            rows, rows, rows, P(), cols, cols, P(), cols, cols, vec, P(), P(), vec, vec, vec, vec, cols,
        ),
        out_specs=(
            rows, rows, vec, P("dp", "tensor"), P("dp", "tensor"), rows, P("dp", "tensor"), cols, vec,
            P(), P(), vec, vec, vec, vec, P("dp", "tensor"),
        ),
        check_vma=False,
    )
```

```python
import jax
import jax.numpy as jnp
from jax import lax
from jax.experimental import pallas as pl
from jax.experimental.pallas import tpu as pltpu
from jax.sharding import PartitionSpec as P

SPAN = 256
HSIZE = 64
LANES = 128
EPSILON = 1e-05
NEG_FILL = -1e30
EXACT = lax.Precision.HIGHEST
F32 = jnp.float32
BF16 = jnp.bfloat16


def mm(left, right):
    return jnp.dot(left, right, preferred_element_type=F32)


def mm_t(left, right):
    return lax.dot_general(left, right, (((1,), (1,)), ((), ())), preferred_element_type=F32)


def t_mm(left, right):
    return lax.dot_general(left, right, (((0,), (0,)), ((), ())), preferred_element_type=F32)


def exact(left, right):
    return jnp.dot(left, right, precision=EXACT, preferred_element_type=F32)


def sigmoid(v):
    return 1.0 / (1.0 + jnp.exp(-v))


def spread(cols, pairs):
    low = lax.broadcasted_iota(jnp.int32, (cols.shape[0], LANES), 1) < HSIZE
    parts = [
        jnp.where(low, cols[:, 2 * p : 2 * p + 1], cols[:, 2 * p + 1 : 2 * p + 2])
        for p in range(pairs)
    ]
    return jnp.concatenate(parts, axis=1)


def gather_mat(inner):
    channel = lax.broadcasted_iota(jnp.int32, (inner, LANES), 0) // HSIZE
    head = lax.broadcasted_iota(jnp.int32, (inner, LANES), 1)
    return (channel == head).astype(F32)


def grid_masks():
    row = lax.broadcasted_iota(jnp.int32, (SPAN, SPAN), 0)
    col = lax.broadcasted_iota(jnp.int32, (SPAN, SPAN), 1)
    return row, col


def conv_fwd(buf, pack, aux):
    out = pack[4:5, :] + buf[8 : 8 + SPAN, :] * pack[3:4, :]
    for j in range(1, 4):
        out = out + buf[8 - j : 8 - j + SPAN, :] * (aux[:, j : j + 1] * pack[3 - j : 4 - j, :])
    return out


def fwd_kernel(
    tok, cot, aux_ref, segr, ng, wg, wv, ws, wst, wo, chp, shp, hp,
    hidden_o, gate_o, vpre_o, cv_o, spre_o, scv_o, z_o, ld_o, ldt_o, yn_o, sin_o, gn_o, stat_o,
    vbuf, sbuf, state,
):
    inner = wg.shape[1]
    pairs = inner // LANES
    state_size = ws.shape[1] // 2

    @pl.when(pl.program_id(0) == 0)
    def _():
        vbuf[0:8, :] = jnp.zeros((8, inner), F32)
        sbuf[0:8, :] = jnp.zeros((8, 2 * state_size), F32)
        state[...] = jnp.zeros_like(state)

    aux = aux_ref[...]
    x = tok[...].astype(F32)
    inv = lax.rsqrt(jnp.mean(x * x, axis=1, keepdims=True) + EPSILON)
    hid = (x * inv * ng[...]).astype(BF16)
    hidden_o[...] = hid
    gate = mm(hid, wg[...])
    gate_o[...] = gate
    vp = mm(hid, wv[...])
    vpre_o[...] = vp
    vbuf[8 : 8 + SPAN, :] = vp
    sp = mm(hid, ws[...])
    spre_o[...] = sp
    sbuf[8 : 8 + SPAN, :] = sp
    z = mm(hid, wst[...]) + hp[0:1, :]
    z_o[...] = z
    gn = mm(cot[...], wo[...])
    gn_o[...] = gn
    scv = conv_fwd(sbuf, shp, aux)
    scv_o[...] = scv
    bc = (scv * sigmoid(scv)).astype(BF16)
    b_low, c_low = bc[:, :state_size], bc[:, state_size:]
    cv = conv_fwd(vbuf, chp, aux)
    cv_o[...] = cv
    vbuf[0:8, :] = vbuf[SPAN : SPAN + 8, :]
    sbuf[0:8, :] = sbuf[SPAN : SPAN + 8, :]
    values = cv * sigmoid(cv)
    dt = jnp.maximum(z, 0.0) + jnp.log1p(jnp.exp(-jnp.abs(z)))
    row, col = grid_masks()
    tri = (row >= col).astype(F32)
    ld = exact(tri, dt * hp[1:2, :])
    ld_o[...] = ld
    ldt = jnp.transpose(ld)[0:8, :]
    ldt_o[...] = ldt
    allowed = (row >= col) & (aux[:, 0:1] == segr[...])
    scores = jnp.where(allowed, mm_t(c_low, b_low), 0.0)
    xs = values * spread(dt, pairs)
    xs_low = xs.astype(BF16)
    ein = jnp.exp(ld) * aux[:, 4:5]
    eout = jnp.exp(ld[SPAN - 1 : SPAN, :] - ld) * aux[:, 5:6]
    ein_x = spread(ein, pairs)
    eout_x = spread(eout, pairs)
    old = state[...]
    sin_o[...] = old
    carried = mm(c_low, old.astype(BF16)) * ein_x
    state[...] = old * ein_x[SPAN - 1 : SPAN, :] + t_mm(b_low, (xs * eout_x).astype(BF16))
    low = lax.broadcasted_iota(jnp.int32, (SPAN, LANES), 1) < HSIZE
    parts = []
    for p in range(pairs):
        pair = xs_low[:, p * LANES : (p + 1) * LANES]
        outs = []
        for h in (2 * p, 2 * p + 1):
            gap = jnp.minimum(ld[:, h : h + 1] - ldt[h : h + 1, :], 0.0)
            outs.append(mm((jnp.exp(gap) * scores).astype(BF16), pair))
        parts.append(jnp.where(low, outs[0], outs[1]))
    yn = jnp.concatenate(parts, axis=1) + carried
    yn_o[...] = yn
    gated = (yn + chp[6:7, :] * values) * (gate * sigmoid(gate))
    squares = jnp.sum(gated * gated, axis=1, keepdims=True)
    dots = jnp.sum(gn * chp[5:6, :] * gated, axis=1, keepdims=True)
    lane = lax.broadcasted_iota(jnp.int32, (SPAN, LANES), 1)
    both = jnp.where(lane == 0, squares, jnp.where(lane == 1, dots, 0.0))
    stat_o[...] = jnp.transpose(both)[0:8, :]


def gate_kernel(
    width, gate_ref, cv_ref, yn, gn_ref, stat, chp, wo, normal_o, dy_o, low_o, gain_o, mixed_o
):
    both = jnp.transpose(jnp.concatenate([stat[...]] * (LANES // 8), axis=0))
    inv = lax.rsqrt(both[:, 0:1] / width + EPSILON)
    mean_dots = both[:, 1:2] / width
    gate = gate_ref[...]
    cv = cv_ref[...]
    gn = gn_ref[...]
    sig = sigmoid(gate)
    act = gate * sig
    mixer = yn[...] + chp[6:7, :] * (cv * sigmoid(cv))
    gated = mixer * act
    normed = gated * inv
    normal = (normed * chp[5:6, :]).astype(BF16)
    normal_o[...] = normal
    mixed_o[...] = mm_t(normal, wo[...]).astype(BF16)
    part = jnp.sum(gn * normed, axis=0, keepdims=True)

    @pl.when(pl.program_id(0) == 0)
    def _():
        gain_o[...] = jnp.zeros_like(gain_o)

    gain_o[0:1, :] += part
    grad_gated = inv * (gn * chp[5:6, :]) - gated * (inv * inv * inv) * mean_dots
    dy_o[...] = grad_gated * act
    low_o[...] = (grad_gated * mixer * (sig * (1.0 + gate * (1.0 - sig)))).astype(BF16)


def bwd_kernel(
    dy_ref, cv_ref, vpre, scv_ref, z_ref, ld_ref, ldt_ref, yn, sin, aux_ref, segr, glow,
    wg, wv, wst, chp, hp,
    vlow_o, slow_o, heads_o, chg_o, hg_o,
    dbuf, dstate,
):
    inner = wg.shape[1]
    pairs = inner // LANES
    state_size = sin.shape[0]

    @pl.when(pl.program_id(0) == 0)
    def _():
        dbuf[SPAN : SPAN + 8, :] = jnp.zeros((8, inner), F32)
        dstate[...] = jnp.zeros_like(dstate)
        chg_o[...] = jnp.zeros_like(chg_o)
        hg_o[...] = jnp.zeros_like(hg_o)

    aux = aux_ref[...]
    dy = dy_ref[...]
    dy_low = dy.astype(BF16)
    scv = scv_ref[...]
    bc = (scv * sigmoid(scv)).astype(BF16)
    b_low, c_low = bc[:, :state_size], bc[:, state_size:]
    cv = cv_ref[...]
    csig = sigmoid(cv)
    values = cv * csig
    z = z_ref[...]
    dt = jnp.maximum(z, 0.0) + jnp.log1p(jnp.exp(-jnp.abs(z)))
    ld = ld_ref[...]
    ldt = ldt_ref[...]
    dt_x = spread(dt, pairs)
    xs = values * dt_x
    xs_low = xs.astype(BF16)
    ein = jnp.exp(ld) * aux[:, 4:5]
    eout = jnp.exp(ld[SPAN - 1 : SPAN, :] - ld) * aux[:, 5:6]
    ein_x = spread(ein, pairs)
    eout_x = spread(eout, pairs)
    row, col = grid_masks()
    allowed = (col >= row) & (aux[:, 0:1] == segr[...])
    mask = allowed.astype(F32)
    scores_t = mm_t(b_low, c_low) * mask
    low = lax.broadcasted_iota(jnp.int32, (SPAN, LANES), 1) < HSIZE
    parts = []
    dscores_t = jnp.zeros((SPAN, SPAN), F32)
    for p in range(pairs):
        cols = slice(p * LANES, (p + 1) * LANES)
        dy_pair = dy_low[:, cols]
        xs_pair = xs_low[:, cols]
        zero = jnp.zeros_like(xs_pair)
        outs = []
        for side, h in enumerate((2 * p, 2 * p + 1)):
            gap = jnp.minimum(ldt[h : h + 1, :] - ld[:, h : h + 1], 0.0)
            decay = jnp.exp(gap)
            outs.append(mm((decay * scores_t).astype(BF16), dy_pair))
            mine = jnp.where(low, xs_pair, zero) if side == 0 else jnp.where(low, zero, xs_pair)
            dscores_t = dscores_t + mm_t(mine, dy_pair) * decay
        parts.append(jnp.where(low, outs[0], outs[1]))
    inside = jnp.concatenate(parts, axis=1)
    dscores_low = (dscores_t * mask).astype(BF16)
    old = sin[...]
    dst = dstate[...]
    dst_low = dst.astype(BF16)
    dye_low = (dy * ein_x).astype(BF16)
    xse_low = (xs * eout_x).astype(BF16)
    db = mm(dscores_low, c_low) + mm_t(xse_low, dst_low)
    dc = t_mm(dscores_low, b_low) + mm_t(dye_low, old.astype(BF16))
    late = mm(b_low, dst_low) * eout_x
    keep = ein_x[SPAN - 1 : SPAN, :]
    dstate[...] = dst * keep + t_mm(c_low, dye_low)
    dxs = inside + late
    collect = gather_mat(inner)
    q = dy_low.astype(F32) * yn[...] - xs_low.astype(F32) * inside
    u = xs * late
    kappa = exact(jnp.sum(old * dst, axis=0, keepdims=True) * keep + jnp.zeros((8, inner), F32), collect)
    da = (
        exact((col >= row).astype(F32), exact(q, collect))
        + exact((row > col).astype(F32), exact(u, collect))
        + kappa[0:1, :]
    )
    rates = hp[1:2, :]
    ddt = da * rates + exact(dxs * values, collect)
    dz = ddt * sigmoid(z)
    slow = dz.astype(BF16)
    slow_o[...] = slow
    skip = exact(jnp.sum(dy * values, axis=0, keepdims=True) + jnp.zeros((8, inner), F32), collect)
    hg_o[0:1, :] += jnp.sum(dz, axis=0, keepdims=True)
    hg_o[1:2, :] += jnp.sum(da * dt, axis=0, keepdims=True) * rates
    hg_o[2:3, :] += skip[0:1, :]
    dcv = (dxs * dt_x + chp[6:7, :] * dy) * (csig * (1.0 + cv * (1.0 - csig)))
    dbuf[0:SPAN, :] = dcv
    vp = vpre[...]
    dv = dcv * chp[3:4, :]
    chg_o[3:4, :] += jnp.sum(dcv * vp, axis=0, keepdims=True)
    chg_o[4:5, :] += jnp.sum(dcv, axis=0, keepdims=True)
    for j in range(1, 4):
        moved = dbuf[j : j + SPAN, :] * aux[:, 8 + j : 9 + j]
        dv = dv + moved * chp[3 - j : 4 - j, :]
        chg_o[3 - j : 4 - j, :] += jnp.sum(moved * vp, axis=0, keepdims=True)
    dbuf[SPAN : SPAN + 8, :] = dbuf[0:8, :]
    vlow = dv.astype(BF16)
    vlow_o[...] = vlow
    back = mm_t(glow[...], wg[...]) + mm_t(vlow, wv[...]) + mm_t(slow, wst[...])
    heads_o[...] = jnp.concatenate([back, db, dc], axis=1).astype(BF16)


def end_kernel(
    summed, scv_ref, spre, aux_ref, tok, cot, ng, ws, shp,
    gtok_o, shlow_o, shg_o, norm_o,
    dbuf,
):
    width = ws.shape[1]

    @pl.when(pl.program_id(0) == 0)
    def _():
        dbuf[SPAN : SPAN + 8, :] = jnp.zeros((8, width), F32)
        shg_o[...] = jnp.zeros_like(shg_o)
        norm_o[...] = jnp.zeros_like(norm_o)

    aux = aux_ref[...]
    scv = scv_ref[...]
    csig = sigmoid(scv)
    dcv = summed[:, tok.shape[1] :].astype(F32) * (csig * (1.0 + scv * (1.0 - csig)))
    dbuf[0:SPAN, :] = dcv
    sp = spre[...]
    ds = dcv * shp[3:4, :]
    shg_o[3:4, :] += jnp.sum(dcv * sp, axis=0, keepdims=True)
    shg_o[4:5, :] += jnp.sum(dcv, axis=0, keepdims=True)
    for j in range(1, 4):
        moved = dbuf[j : j + SPAN, :] * aux[:, 8 + j : 9 + j]
        ds = ds + moved * shp[3 - j : 4 - j, :]
        shg_o[3 - j : 4 - j, :] += jnp.sum(moved * sp, axis=0, keepdims=True)
    dbuf[SPAN : SPAN + 8, :] = dbuf[0:8, :]
    shlow = ds.astype(BF16)
    shlow_o[...] = shlow
    grad_hidden = summed[:, : tok.shape[1]].astype(F32) + mm_t(shlow, ws[...])
    x = tok[...].astype(F32)
    inv = lax.rsqrt(jnp.mean(x * x, axis=1, keepdims=True) + EPSILON)
    normed = x * inv
    scaled = grad_hidden * ng[...]
    norm_o[0:1, :] += jnp.sum(grad_hidden * normed, axis=0, keepdims=True)
    mean = jnp.mean(scaled * normed, axis=1, keepdims=True)
    gtok_o[...] = (inv * (scaled - normed * mean) + cot[...].astype(F32)).astype(BF16)


MESH = pl.DeviceIdType.MESH
PIECES = 4


def prep_kernel(seg, aux_o, segr_o):
    length = seg.shape[1]
    ids = seg[...].astype(F32)
    segr_o[...] = ids
    wide = ids + jnp.zeros((8, length), F32)
    lane = lax.broadcasted_iota(jnp.int32, (8, length), 1)
    row = lax.broadcasted_iota(jnp.int32, (8, length), 0)
    ends = [
        ids[:, start + SPAN - 1 : start + SPAN] + jnp.zeros((8, SPAN), F32)
        for start in range(0, length, SPAN)
    ]
    last = jnp.concatenate(ends, axis=1)
    before = jnp.concatenate([jnp.full((8, SPAN), -1.0, F32)] + ends[:-1], axis=1)
    first = jnp.where(row == 0, wide, 0.0)
    first = jnp.where((row == 4) & (wide == before), 1.0, first)
    first = jnp.where((row == 5) & (wide == last), 1.0, first)
    second = jnp.zeros((8, length), F32)
    for j in range(1, 4):
        back = (pltpu.roll(wide, j, 1) == wide) & (lane >= j)
        ahead = (pltpu.roll(wide, length - j, 1) == wide) & (lane < length - j)
        first = jnp.where((row == j) & back, 1.0, first)
        second = jnp.where((row == j) & ahead, 1.0, second)
    rest = jnp.zeros((LANES - 16, length), F32)
    aux_o[...] = jnp.transpose(jnp.concatenate([first, second, rest], axis=0))


def small_sum(x, axis, collective_id):
    count = lax.axis_size(axis)

    def body(x_ref, out_ref, slots, send, recv):
        me = lax.axis_index(axis)
        barrier = pltpu.get_barrier_semaphore()
        for k in range(1, count):
            peer = lax.rem(me + k, count)
            pl.semaphore_signal(barrier, inc=1, device_id={axis: peer}, device_id_type=MESH)
        pl.semaphore_wait(barrier, count - 1)
        copies = []
        for k in range(1, count):
            copies.append(
                pltpu.make_async_remote_copy(
                    src_ref=x_ref,
                    dst_ref=slots.at[k],
                    send_sem=send.at[k],
                    recv_sem=recv.at[k],
                    device_id={axis: lax.rem(me + k, count)},
                    device_id_type=MESH,
                )
            )
            copies[-1].start()
        slots[0] = x_ref[...]
        for copy in copies:
            copy.wait()
        total = slots[me]
        for source in range(1, count):
            total = total + slots[lax.rem(me - source + count, count)]
        out_ref[...] = total

    return pl.pallas_call(
        body,
        in_specs=[pl.BlockSpec(memory_space=pltpu.VMEM)],
        out_specs=pl.BlockSpec(memory_space=pltpu.VMEM),
        out_shape=jax.ShapeDtypeStruct(x.shape, x.dtype),
        scratch_shapes=[
            pltpu.VMEM((count,) + x.shape, x.dtype),
            pltpu.SemaphoreType.DMA((count,)),
            pltpu.SemaphoreType.DMA((count,)),
        ],
        compiler_params=pltpu.CompilerParams(collective_id=collective_id, has_side_effects=True),
        name="small_sum_" + axis,
    )(x)


def wide_sum(x, axis, collective_id):
    groups = lax.axis_size(axis) // 2
    length, width = x.shape
    half = length // 2
    rows = half // PIECES

    def body(x_ref, out_ref, near, far, send_a, recv_a, send_b, recv_b, send_c, recv_c):
        me = lax.axis_index(axis)
        side = lax.rem(me, 2)
        chip = me // 2
        sibling = 2 * chip + 1 - side
        mates = [2 * lax.rem(chip + q, groups) + side for q in range(1, groups)]
        barrier = pltpu.get_barrier_semaphore()
        for peer in [sibling] + mates:
            pl.semaphore_signal(barrier, inc=1, device_id={axis: peer}, device_id_type=MESH)
        pl.semaphore_wait(barrier, groups)
        first, second, third = [], [], []

        def part(which, k):
            return pl.ds(pl.multiple_of(which * half + k * rows, rows), rows)

        for k in range(PIECES):
            first.append(
                pltpu.make_async_remote_copy(
                    src_ref=x_ref.at[part(1 - side, k)],
                    dst_ref=near.at[k],
                    send_sem=send_a.at[k],
                    recv_sem=recv_a.at[k],
                    device_id={axis: sibling},
                    device_id_type=MESH,
                )
            )
            first[-1].start()
        for k in range(PIECES):
            first[k].wait_recv()
            mine = x_ref[part(side, k), :].astype(F32) + near[k].astype(F32)
            far[0, k] = mine.astype(BF16)
            for q in range(1, groups):
                second.append(
                    pltpu.make_async_remote_copy(
                        src_ref=far.at[0, k],
                        dst_ref=far.at[q, k],
                        send_sem=send_b.at[q, k],
                        recv_sem=recv_b.at[q, k],
                        device_id={axis: mates[q - 1]},
                        device_id_type=MESH,
                    )
                )
                second[-1].start()
        for k in range(PIECES):
            for q in range(1, groups):
                second[k * (groups - 1) + q - 1].wait_recv()
            total = far[chip, k].astype(F32)
            for source in range(1, groups):
                total = total + far[lax.rem(chip - source + groups, groups), k].astype(F32)
            out_ref[part(side, k), :] = total.astype(BF16)
            third.append(
                pltpu.make_async_remote_copy(
                    src_ref=out_ref.at[part(side, k)],
                    dst_ref=out_ref.at[part(side, k)],
                    send_sem=send_c.at[k],
                    recv_sem=recv_c.at[k],
                    device_id={axis: sibling},
                    device_id_type=MESH,
                )
            )
            third[-1].start()
        for copy in first + second:
            copy.wait_send()
        for copy in third:
            copy.wait()

    dma = pltpu.SemaphoreType.DMA
    return pl.pallas_call(
        body,
        in_specs=[pl.BlockSpec(memory_space=pltpu.VMEM)],
        out_specs=pl.BlockSpec(memory_space=pltpu.VMEM),
        out_shape=jax.ShapeDtypeStruct(x.shape, x.dtype),
        scratch_shapes=[
            pltpu.VMEM((PIECES, rows, width), BF16),
            pltpu.VMEM((groups, PIECES, rows, width), BF16),
            dma((PIECES,)), dma((PIECES,)), dma((groups, PIECES)), dma((groups, PIECES)),
            dma((PIECES,)), dma((PIECES,)),
        ],
        compiler_params=pltpu.CompilerParams(
            collective_id=collective_id, has_side_effects=True, vmem_limit_bytes=40 * 1024 * 1024
        ),
        name="wide_sum",
    )(x)


def call(body, blocks, ins, outs, scratch, backward, name):
    def spec(shape, kind):
        if kind == "whole":
            return pl.BlockSpec(shape, lambda i: (0,) * len(shape))
        if kind == "lanes":
            block = (shape[0], shape[1] // blocks)
            return pl.BlockSpec(block, (lambda i: (0, blocks - 1 - i)) if backward else (lambda i: (0, i)))
        block = (shape[0] // blocks, shape[1])
        return pl.BlockSpec(block, (lambda i: (blocks - 1 - i, 0)) if backward else (lambda i: (i, 0)))

    return pl.pallas_call(
        body,
        grid=(blocks,),
        in_specs=[spec(a.shape, kind) for a, kind in ins],
        out_specs=[spec(shape, kind) for shape, _, kind in outs],
        out_shape=[jax.ShapeDtypeStruct(shape, dtype) for shape, dtype, _ in outs],
        scratch_shapes=scratch,
        compiler_params=pltpu.CompilerParams(
            dimension_semantics=("arbitrary",), vmem_limit_bytes=60 * 1024 * 1024
        ),
        name=name,
    )(*[a for a, _ in ins])


def pad_rows(parts, width):
    rows = [jnp.pad(p.astype(F32), ((0, 0), (0, width - p.shape[1]))) for p in parts]
    used = sum(r.shape[0] for r in rows)
    return jnp.concatenate(rows + [jnp.zeros((8 - used, width), F32)], axis=0)


def per_device(
    tokens, cotangent, segments, norm_gain, gate_proj, value_proj, shared_proj, step_proj,
    conv_value, bias_value, conv_shared, bias_shared, step_bias, decay_log, skip_gain,
    gate_gain, out_proj,
):
    tp_count = lax.axis_size("tensor")
    length, width = tokens.shape
    inner = gate_proj.shape[1]
    heads = step_proj.shape[1]
    shared_width = shared_proj.shape[1]
    state_size = shared_width // 2
    blocks = length // SPAN
    aux, segr = pl.pallas_call(
        prep_kernel,
        out_shape=[
            jax.ShapeDtypeStruct((length, LANES), F32),
            jax.ShapeDtypeStruct((1, length), F32),
        ],
        name="prep_step",
    )(segments)
    ng = norm_gain[None, :]
    wst = jnp.pad(step_proj, ((0, 0), (0, LANES - heads)))
    chp = pad_rows(
        [conv_value, bias_value[None], gate_gain[None], jnp.repeat(skip_gain, HSIZE)[None]], inner
    )
    shp = pad_rows([conv_shared, bias_shared[None]], shared_width)
    hp = pad_rows([step_bias[None], -jnp.exp(decay_log)[None]], LANES)

    (
        hidden, gate_pre, value_pre, conv_out, shared_pre, shared_conv, z, ld, ldt, yn, sin, gn, stat,
    ) = call(
        fwd_kernel,
        blocks,
        [
            (tokens, "rows"), (cotangent, "rows"), (aux, "rows"), (segr, "lanes"), (ng, "whole"),
            (gate_proj, "whole"), (value_proj, "whole"), (shared_proj, "whole"), (wst, "whole"),
            (out_proj, "whole"), (chp, "whole"), (shp, "whole"), (hp, "whole"),
        ],
        [
            ((length, width), BF16, "rows"),
            ((length, inner), F32, "rows"),
            ((length, inner), F32, "rows"),
            ((length, inner), F32, "rows"),
            ((length, shared_width), F32, "rows"),
            ((length, shared_width), F32, "rows"),
            ((length, LANES), F32, "rows"),
            ((length, LANES), F32, "rows"),
            ((8, length), F32, "lanes"),
            ((length, inner), F32, "rows"),
            ((blocks * state_size, inner), F32, "rows"),
            ((length, inner), F32, "rows"),
            ((8, length), F32, "lanes"),
        ],
        [
            pltpu.VMEM((SPAN + 8, inner), F32),
            pltpu.VMEM((SPAN + 8, shared_width), F32),
            pltpu.VMEM((state_size, inner), F32),
        ],
        False,
        "fwd_scan",
    )
    stat = small_sum(stat, "tensor", 0)
    total_inner = float(inner * tp_count)

    def gate_body(*refs):
        gate_kernel(total_inner, *refs)

    normal_out, dy, gate_low, gain_part, mixed_part = call(
        gate_body,
        blocks,
        [
            (gate_pre, "rows"), (conv_out, "rows"), (yn, "rows"), (gn, "rows"), (stat, "lanes"),
            (chp, "whole"), (out_proj, "whole"),
        ],
        [
            ((length, inner), BF16, "rows"),
            ((length, inner), F32, "rows"),
            ((length, inner), BF16, "rows"),
            ((8, inner), F32, "whole"),
            ((length, width), BF16, "rows"),
        ],
        [],
        False,
        "gate_step",
    )
    mixed = lax.psum(mixed_part, "tensor")
    value_low, step_low, heads_part, ch_grads, head_grads = call(
        bwd_kernel,
        blocks,
        [
            (dy, "rows"), (conv_out, "rows"), (value_pre, "rows"), (shared_conv, "rows"),
            (z, "rows"), (ld, "rows"), (ldt, "lanes"), (yn, "rows"), (sin, "rows"),
            (aux, "rows"), (segr, "lanes"), (gate_low, "rows"), (gate_proj, "whole"),
            (value_proj, "whole"), (wst, "whole"), (chp, "whole"), (hp, "whole"),
        ],
        [
            ((length, inner), BF16, "rows"),
            ((length, LANES), BF16, "rows"),
            ((length, width + shared_width), BF16, "rows"),
            ((8, inner), F32, "whole"),
            ((8, LANES), F32, "whole"),
        ],
        [pltpu.VMEM((SPAN + 8, inner), F32), pltpu.VMEM((state_size, inner), F32)],
        True,
        "bwd_scan",
    )
    early = lax.psum_scatter(
        jnp.concatenate(
            [
                t_mm(hidden, jnp.concatenate([gate_low, value_low, step_low], axis=1)),
                t_mm(cotangent, normal_out),
            ],
            axis=1,
        ).astype(BF16),
        "dp",
        scatter_dimension=0,
        tiled=True,
    ).astype(F32)
    summed = wide_sum(heads_part, "tensor", 1)
    grad_tokens, shared_low, sh_grads, norm_part = call(
        end_kernel,
        blocks,
        [
            (summed, "rows"), (shared_conv, "rows"), (shared_pre, "rows"), (aux, "rows"),
            (tokens, "rows"), (cotangent, "rows"),
            (ng, "whole"), (shared_proj, "whole"), (shp, "whole"),
        ],
        [
            ((length, width), BF16, "rows"),
            ((length, shared_width), BF16, "rows"),
            ((8, shared_width), F32, "whole"),
            ((8, width), F32, "whole"),
        ],
        [pltpu.VMEM((SPAN + 8, shared_width), F32)],
        True,
        "end_step",
    )
    late = lax.psum_scatter(
        t_mm(hidden, shared_low).astype(BF16),
        "dp",
        scatter_dimension=0,
        tiled=True,
    ).astype(F32)
    col_width = width // tp_count
    norm_mine = lax.dynamic_slice_in_dim(
        norm_part[0], lax.axis_index("tensor") * col_width, col_width, 0
    )
    packed = jnp.concatenate(
        [
            norm_mine, ch_grads[:5].reshape(-1), sh_grads[:5].reshape(-1),
            head_grads[:3].reshape(-1), gain_part[0],
        ]
    )
    packed = packed.reshape(-1, LANES)
    packed = jnp.pad(packed, ((0, -packed.shape[0] % 8), (0, 0)))
    packed = small_sum(packed, "dp", 2).reshape(-1)
    sizes = [col_width, 5 * inner, 5 * shared_width, 3 * LANES, inner]
    pieces, start = [], 0
    for size in sizes:
        pieces.append(packed[start : start + size])
        start += size
    channel = pieces[1].reshape(5, inner)
    shared = pieces[2].reshape(5, shared_width)
    per_head = pieces[3].reshape(3, LANES)[:, :heads]
    result = (tokens.astype(F32) + mixed.astype(F32)).astype(BF16)
    return (
        result,
        grad_tokens,
        pieces[0],
        early[:, :inner],
        early[:, inner : 2 * inner],
        late,
        early[:, 2 * inner : 2 * inner + heads],
        channel[:4],
        channel[4],
        shared[:4],
        shared[4],
        per_head[0],
        per_head[1],
        per_head[2],
        pieces[4],
        early[:, 2 * inner + LANES :],
    )


def solution(mesh):
    rows, cols, vec = P("dp", None), P(None, "tensor"), P("tensor")
    return jax.shard_map(
        per_device,
        mesh=mesh,
        in_specs=(
            rows, rows, rows, P(), cols, cols, P(), cols, cols, vec, P(), P(), vec, vec, vec, vec, cols,
        ),
        out_specs=(
            rows, rows, vec, P("dp", "tensor"), P("dp", "tensor"), rows, P("dp", "tensor"), cols, vec,
            P(), P(), vec, vec, vec, vec, P("dp", "tensor"),
        ),
        check_vma=False,
    )
```

```python
import jax
import jax.numpy as jnp
from jax import lax
from jax.experimental import pallas as pl
from jax.experimental.pallas import tpu as pltpu
from jax.sharding import PartitionSpec as P

SPAN = 256
HSIZE = 64
LANES = 128
EPSILON = 1e-05
NEG_FILL = -1e30
EXACT = lax.Precision.HIGHEST
F32 = jnp.float32
BF16 = jnp.bfloat16


def mm(left, right):
    return jnp.dot(left, right, preferred_element_type=F32)


def mm_t(left, right):
    return lax.dot_general(left, right, (((1,), (1,)), ((), ())), preferred_element_type=F32)


def t_mm(left, right):
    return lax.dot_general(left, right, (((0,), (0,)), ((), ())), preferred_element_type=F32)


def exact(left, right):
    return jnp.dot(left, right, precision=EXACT, preferred_element_type=F32)


def sigmoid(v):
    return 1.0 / (1.0 + jnp.exp(-v))


def spread(cols, pairs):
    low = lax.broadcasted_iota(jnp.int32, (cols.shape[0], LANES), 1) < HSIZE
    parts = [
        jnp.where(low, cols[:, 2 * p : 2 * p + 1], cols[:, 2 * p + 1 : 2 * p + 2])
        for p in range(pairs)
    ]
    return jnp.concatenate(parts, axis=1)


def gather_mat(inner):
    channel = lax.broadcasted_iota(jnp.int32, (inner, LANES), 0) // HSIZE
    head = lax.broadcasted_iota(jnp.int32, (inner, LANES), 1)
    return (channel == head).astype(F32)


def grid_masks():
    row = lax.broadcasted_iota(jnp.int32, (SPAN, SPAN), 0)
    col = lax.broadcasted_iota(jnp.int32, (SPAN, SPAN), 1)
    return row, col


def conv_fwd(buf, pack, aux):
    out = pack[4:5, :] + buf[8 : 8 + SPAN, :] * pack[3:4, :]
    for j in range(1, 4):
        out = out + buf[8 - j : 8 - j + SPAN, :] * (aux[:, j : j + 1] * pack[3 - j : 4 - j, :])
    return out


def fwd_kernel(
    tok, cot, aux_ref, segr, ng, wg, wv, ws, wst, wo, chp, shp, hp,
    hidden_o, gate_o, vpre_o, cv_o, spre_o, scv_o, z_o, ld_o, ldt_o, yn_o, sin_o, gn_o, stat_o,
    vbuf, sbuf, state,
):
    inner = wg.shape[1]
    pairs = inner // LANES
    state_size = ws.shape[1] // 2

    @pl.when(pl.program_id(0) == 0)
    def _():
        vbuf[0:8, :] = jnp.zeros((8, inner), F32)
        sbuf[0:8, :] = jnp.zeros((8, 2 * state_size), F32)
        state[...] = jnp.zeros_like(state)

    aux = aux_ref[...]
    x = tok[...].astype(F32)
    inv = lax.rsqrt(jnp.mean(x * x, axis=1, keepdims=True) + EPSILON)
    hid = (x * inv * ng[...]).astype(BF16)
    hidden_o[...] = hid
    gate = mm(hid, wg[...])
    gate_o[...] = gate
    vp = mm(hid, wv[...])
    vpre_o[...] = vp
    vbuf[8 : 8 + SPAN, :] = vp
    sp = mm(hid, ws[...])
    spre_o[...] = sp
    sbuf[8 : 8 + SPAN, :] = sp
    z = mm(hid, wst[...]) + hp[0:1, :]
    z_o[...] = z
    gn = mm(cot[...], wo[...])
    gn_o[...] = gn
    scv = conv_fwd(sbuf, shp, aux)
    scv_o[...] = scv
    bc = (scv * sigmoid(scv)).astype(BF16)
    b_low, c_low = bc[:, :state_size], bc[:, state_size:]
    cv = conv_fwd(vbuf, chp, aux)
    cv_o[...] = cv
    vbuf[0:8, :] = vbuf[SPAN : SPAN + 8, :]
    sbuf[0:8, :] = sbuf[SPAN : SPAN + 8, :]
    values = cv * sigmoid(cv)
    dt = jnp.maximum(z, 0.0) + jnp.log1p(jnp.exp(-jnp.abs(z)))
    row, col = grid_masks()
    tri = (row >= col).astype(F32)
    ld = exact(tri, dt * hp[1:2, :])
    ld_o[...] = ld
    ldt = jnp.transpose(ld)[0:8, :]
    ldt_o[...] = ldt
    allowed = (row >= col) & (aux[:, 0:1] == segr[...])
    scores = jnp.where(allowed, mm_t(c_low, b_low), 0.0)
    xs = values * spread(dt, pairs)
    xs_low = xs.astype(BF16)
    ein = jnp.exp(ld) * aux[:, 4:5]
    eout = jnp.exp(ld[SPAN - 1 : SPAN, :] - ld) * aux[:, 5:6]
    ein_x = spread(ein, pairs)
    eout_x = spread(eout, pairs)
    old = state[...]
    sin_o[...] = old
    carried = mm(c_low, old.astype(BF16)) * ein_x
    state[...] = old * ein_x[SPAN - 1 : SPAN, :] + t_mm(b_low, (xs * eout_x).astype(BF16))
    low = lax.broadcasted_iota(jnp.int32, (SPAN, LANES), 1) < HSIZE
    parts = []
    for p in range(pairs):
        pair = xs_low[:, p * LANES : (p + 1) * LANES]
        outs = []
        for h in (2 * p, 2 * p + 1):
            gap = jnp.minimum(ld[:, h : h + 1] - ldt[h : h + 1, :], 0.0)
            outs.append(mm((jnp.exp(gap) * scores).astype(BF16), pair))
        parts.append(jnp.where(low, outs[0], outs[1]))
    yn = jnp.concatenate(parts, axis=1) + carried
    yn_o[...] = yn
    gated = (yn + chp[6:7, :] * values) * (gate * sigmoid(gate))
    squares = jnp.sum(gated * gated, axis=1, keepdims=True)
    dots = jnp.sum(gn * chp[5:6, :] * gated, axis=1, keepdims=True)
    lane = lax.broadcasted_iota(jnp.int32, (SPAN, LANES), 1)
    both = jnp.where(lane == 0, squares, jnp.where(lane == 1, dots, 0.0))
    stat_o[...] = jnp.transpose(both)[0:8, :]


def gate_kernel(
    width, gate_ref, cv_ref, yn, gn_ref, stat, chp, wo, normal_o, dy_o, low_o, gain_o, mixed_o
):
    both = jnp.transpose(jnp.concatenate([stat[...]] * (LANES // 8), axis=0))
    inv = lax.rsqrt(both[:, 0:1] / width + EPSILON)
    mean_dots = both[:, 1:2] / width
    gate = gate_ref[...]
    cv = cv_ref[...]
    gn = gn_ref[...]
    sig = sigmoid(gate)
    act = gate * sig
    mixer = yn[...] + chp[6:7, :] * (cv * sigmoid(cv))
    gated = mixer * act
    normed = gated * inv
    normal = (normed * chp[5:6, :]).astype(BF16)
    normal_o[...] = normal
    mixed_o[...] = mm_t(normal, wo[...]).astype(BF16)
    part = jnp.sum(gn * normed, axis=0, keepdims=True)

    @pl.when(pl.program_id(0) == 0)
    def _():
        gain_o[...] = jnp.zeros_like(gain_o)

    gain_o[0:1, :] += part
    grad_gated = inv * (gn * chp[5:6, :]) - gated * (inv * inv * inv) * mean_dots
    dy_o[...] = grad_gated * act
    low_o[...] = (grad_gated * mixer * (sig * (1.0 + gate * (1.0 - sig)))).astype(BF16)


def bwd_kernel(
    dy_ref, cv_ref, vpre, scv_ref, z_ref, ld_ref, ldt_ref, yn, sin, aux_ref, segr, glow,
    wg, wv, wst, chp, hp,
    vlow_o, slow_o, heads_o, dbc_o, chg_o, hg_o,
    dbuf, dstate,
):
    inner = wg.shape[1]
    pairs = inner // LANES
    state_size = sin.shape[0]

    @pl.when(pl.program_id(0) == 0)
    def _():
        dbuf[SPAN : SPAN + 8, :] = jnp.zeros((8, inner), F32)
        dstate[...] = jnp.zeros_like(dstate)
        chg_o[...] = jnp.zeros_like(chg_o)
        hg_o[...] = jnp.zeros_like(hg_o)

    aux = aux_ref[...]
    dy = dy_ref[...]
    dy_low = dy.astype(BF16)
    scv = scv_ref[...]
    bc = (scv * sigmoid(scv)).astype(BF16)
    b_low, c_low = bc[:, :state_size], bc[:, state_size:]
    cv = cv_ref[...]
    csig = sigmoid(cv)
    values = cv * csig
    z = z_ref[...]
    dt = jnp.maximum(z, 0.0) + jnp.log1p(jnp.exp(-jnp.abs(z)))
    ld = ld_ref[...]
    ldt = ldt_ref[...]
    dt_x = spread(dt, pairs)
    xs = values * dt_x
    xs_low = xs.astype(BF16)
    ein = jnp.exp(ld) * aux[:, 4:5]
    eout = jnp.exp(ld[SPAN - 1 : SPAN, :] - ld) * aux[:, 5:6]
    ein_x = spread(ein, pairs)
    eout_x = spread(eout, pairs)
    row, col = grid_masks()
    allowed = (col >= row) & (aux[:, 0:1] == segr[...])
    mask = allowed.astype(F32)
    scores_t = mm_t(b_low, c_low) * mask
    low = lax.broadcasted_iota(jnp.int32, (SPAN, LANES), 1) < HSIZE
    parts = []
    dscores_t = jnp.zeros((SPAN, SPAN), F32)
    for p in range(pairs):
        cols = slice(p * LANES, (p + 1) * LANES)
        dy_pair = dy_low[:, cols]
        xs_pair = xs_low[:, cols]
        zero = jnp.zeros_like(xs_pair)
        outs = []
        for side, h in enumerate((2 * p, 2 * p + 1)):
            gap = jnp.minimum(ldt[h : h + 1, :] - ld[:, h : h + 1], 0.0)
            decay = jnp.exp(gap)
            outs.append(mm((decay * scores_t).astype(BF16), dy_pair))
            mine = jnp.where(low, xs_pair, zero) if side == 0 else jnp.where(low, zero, xs_pair)
            dscores_t = dscores_t + mm_t(mine, dy_pair) * decay
        parts.append(jnp.where(low, outs[0], outs[1]))
    inside = jnp.concatenate(parts, axis=1)
    dscores_low = (dscores_t * mask).astype(BF16)
    old = sin[...]
    dst = dstate[...]
    dst_low = dst.astype(BF16)
    dye_low = (dy * ein_x).astype(BF16)
    xse_low = (xs * eout_x).astype(BF16)
    db = mm(dscores_low, c_low) + mm_t(xse_low, dst_low)
    dc = t_mm(dscores_low, b_low) + mm_t(dye_low, old.astype(BF16))
    late = mm(b_low, dst_low) * eout_x
    keep = ein_x[SPAN - 1 : SPAN, :]
    dstate[...] = dst * keep + t_mm(c_low, dye_low)
    dxs = inside + late
    collect = gather_mat(inner)
    q = dy_low.astype(F32) * yn[...] - xs_low.astype(F32) * inside
    u = xs * late
    kappa = exact(jnp.sum(old * dst, axis=0, keepdims=True) * keep + jnp.zeros((8, inner), F32), collect)
    da = (
        exact((col >= row).astype(F32), exact(q, collect))
        + exact((row > col).astype(F32), exact(u, collect))
        + kappa[0:1, :]
    )
    rates = hp[1:2, :]
    ddt = da * rates + exact(dxs * values, collect)
    dz = ddt * sigmoid(z)
    slow = dz.astype(BF16)
    slow_o[...] = slow
    skip = exact(jnp.sum(dy * values, axis=0, keepdims=True) + jnp.zeros((8, inner), F32), collect)
    hg_o[0:1, :] += jnp.sum(dz, axis=0, keepdims=True)
    hg_o[1:2, :] += jnp.sum(da * dt, axis=0, keepdims=True) * rates
    hg_o[2:3, :] += skip[0:1, :]
    dcv = (dxs * dt_x + chp[6:7, :] * dy) * (csig * (1.0 + cv * (1.0 - csig)))
    dbuf[0:SPAN, :] = dcv
    vp = vpre[...]
    dv = dcv * chp[3:4, :]
    chg_o[3:4, :] += jnp.sum(dcv * vp, axis=0, keepdims=True)
    chg_o[4:5, :] += jnp.sum(dcv, axis=0, keepdims=True)
    for j in range(1, 4):
        moved = dbuf[j : j + SPAN, :] * aux[:, 8 + j : 9 + j]
        dv = dv + moved * chp[3 - j : 4 - j, :]
        chg_o[3 - j : 4 - j, :] += jnp.sum(moved * vp, axis=0, keepdims=True)
    dbuf[SPAN : SPAN + 8, :] = dbuf[0:8, :]
    vlow = dv.astype(BF16)
    vlow_o[...] = vlow
    back = mm_t(glow[...], wg[...]) + mm_t(vlow, wv[...]) + mm_t(slow, wst[...])
    heads_o[...] = back.astype(BF16)
    dbc_o[...] = jnp.concatenate([db, dc], axis=1)


def end_kernel(
    heads_sum, dbc, scv_ref, spre, aux_ref, tok, cot, ng, ws, shp,
    gtok_o, shlow_o, shg_o, norm_o,
    dbuf,
):
    width = ws.shape[1]

    @pl.when(pl.program_id(0) == 0)
    def _():
        dbuf[SPAN : SPAN + 8, :] = jnp.zeros((8, width), F32)
        shg_o[...] = jnp.zeros_like(shg_o)
        norm_o[...] = jnp.zeros_like(norm_o)

    aux = aux_ref[...]
    scv = scv_ref[...]
    csig = sigmoid(scv)
    dcv = dbc[...] * (csig * (1.0 + scv * (1.0 - csig)))
    dbuf[0:SPAN, :] = dcv
    sp = spre[...]
    ds = dcv * shp[3:4, :]
    shg_o[3:4, :] += jnp.sum(dcv * sp, axis=0, keepdims=True)
    shg_o[4:5, :] += jnp.sum(dcv, axis=0, keepdims=True)
    for j in range(1, 4):
        moved = dbuf[j : j + SPAN, :] * aux[:, 8 + j : 9 + j]
        ds = ds + moved * shp[3 - j : 4 - j, :]
        shg_o[3 - j : 4 - j, :] += jnp.sum(moved * sp, axis=0, keepdims=True)
    dbuf[SPAN : SPAN + 8, :] = dbuf[0:8, :]
    shlow = ds.astype(BF16)
    shlow_o[...] = shlow
    grad_hidden = heads_sum[...].astype(F32) + mm_t(shlow, ws[...])
    x = tok[...].astype(F32)
    inv = lax.rsqrt(jnp.mean(x * x, axis=1, keepdims=True) + EPSILON)
    normed = x * inv
    scaled = grad_hidden * ng[...]
    norm_o[0:1, :] += jnp.sum(grad_hidden * normed, axis=0, keepdims=True)
    mean = jnp.mean(scaled * normed, axis=1, keepdims=True)
    gtok_o[...] = (inv * (scaled - normed * mean) + cot[...].astype(F32)).astype(BF16)


MESH = pl.DeviceIdType.MESH
PIECES = 4


def prep_kernel(seg, aux_o, segr_o):
    length = seg.shape[1]
    ids = seg[...].astype(F32)
    segr_o[...] = ids
    wide = ids + jnp.zeros((8, length), F32)
    lane = lax.broadcasted_iota(jnp.int32, (8, length), 1)
    row = lax.broadcasted_iota(jnp.int32, (8, length), 0)
    ends = [
        ids[:, start + SPAN - 1 : start + SPAN] + jnp.zeros((8, SPAN), F32)
        for start in range(0, length, SPAN)
    ]
    last = jnp.concatenate(ends, axis=1)
    before = jnp.concatenate([jnp.full((8, SPAN), -1.0, F32)] + ends[:-1], axis=1)
    first = jnp.where(row == 0, wide, 0.0)
    first = jnp.where((row == 4) & (wide == before), 1.0, first)
    first = jnp.where((row == 5) & (wide == last), 1.0, first)
    second = jnp.zeros((8, length), F32)
    for j in range(1, 4):
        back = (pltpu.roll(wide, j, 1) == wide) & (lane >= j)
        ahead = (pltpu.roll(wide, length - j, 1) == wide) & (lane < length - j)
        first = jnp.where((row == j) & back, 1.0, first)
        second = jnp.where((row == j) & ahead, 1.0, second)
    rest = jnp.zeros((LANES - 16, length), F32)
    aux_o[...] = jnp.transpose(jnp.concatenate([first, second, rest], axis=0))


def small_sum(x, axis, collective_id):
    count = lax.axis_size(axis)

    def body(x_ref, out_ref, slots, send, recv):
        me = lax.axis_index(axis)
        barrier = pltpu.get_barrier_semaphore()
        for k in range(1, count):
            peer = lax.rem(me + k, count)
            pl.semaphore_signal(barrier, inc=1, device_id={axis: peer}, device_id_type=MESH)
        pl.semaphore_wait(barrier, count - 1)
        copies = []
        for k in range(1, count):
            copies.append(
                pltpu.make_async_remote_copy(
                    src_ref=x_ref,
                    dst_ref=slots.at[k],
                    send_sem=send.at[k],
                    recv_sem=recv.at[k],
                    device_id={axis: lax.rem(me + k, count)},
                    device_id_type=MESH,
                )
            )
            copies[-1].start()
        slots[0] = x_ref[...]
        for copy in copies:
            copy.wait()
        total = slots[me]
        for source in range(1, count):
            total = total + slots[lax.rem(me - source + count, count)]
        out_ref[...] = total

    return pl.pallas_call(
        body,
        in_specs=[pl.BlockSpec(memory_space=pltpu.VMEM)],
        out_specs=pl.BlockSpec(memory_space=pltpu.VMEM),
        out_shape=jax.ShapeDtypeStruct(x.shape, x.dtype),
        scratch_shapes=[
            pltpu.VMEM((count,) + x.shape, x.dtype),
            pltpu.SemaphoreType.DMA((count,)),
            pltpu.SemaphoreType.DMA((count,)),
        ],
        compiler_params=pltpu.CompilerParams(collective_id=collective_id, has_side_effects=True),
        name="small_sum_" + axis,
    )(x)


def wide_sum(arrays, axis, collective_id, micros):
    groups = lax.axis_size(axis) // 2
    half = arrays[0].shape[0] // 2
    rows = half // PIECES
    count = len(arrays)
    items = [(k, n) for k in range(PIECES) for n in range(count)]

    def body(*refs):
        xs, outs = refs[:count], refs[count : 2 * count]
        nears, fars = refs[2 * count : 3 * count], refs[3 * count : 4 * count]
        send_a, recv_a, send_b, recv_b, send_c, recv_c = refs[4 * count :]
        me = lax.axis_index(axis)
        side = lax.rem(me, 2)
        chip = me // 2
        sibling = 2 * chip + 1 - side
        mates = [2 * lax.rem(chip + q, groups) + side for q in range(1, groups)]
        barrier = pltpu.get_barrier_semaphore()
        for peer in [sibling] + mates:
            pl.semaphore_signal(barrier, inc=1, device_id={axis: peer}, device_id_type=MESH)
        pl.semaphore_wait(barrier, groups)

        def part(which, k):
            return pl.ds(pl.multiple_of(which * half + k * rows, rows), rows)

        def remote(src, dst, send, recv, peer):
            copy = pltpu.make_async_remote_copy(
                src_ref=src,
                dst_ref=dst,
                send_sem=send,
                recv_sem=recv,
                device_id={axis: peer},
                device_id_type=MESH,
            )
            copy.start()
            return copy

        first, second, third = {}, {}, {}
        for k, n in items:
            first[k, n] = remote(
                xs[n].at[part(1 - side, k)], nears[n].at[k], send_a.at[n, k], recv_a.at[n, k], sibling
            )
        for k, n in items:
            first[k, n].wait_recv()
            mine = xs[n][part(side, k), :].astype(F32) + nears[n][k].astype(F32)
            fars[n][0, k] = mine.astype(fars[n].dtype)
            for q in range(1, groups):
                second[k, n, q] = remote(
                    fars[n].at[0, k], fars[n].at[q, k], send_b.at[n, q, k], recv_b.at[n, q, k],
                    mates[q - 1],
                )
        for k, n in items:
            for q in range(1, groups):
                second[k, n, q].wait_recv()
            total = fars[n][chip, k].astype(F32)
            for source in range(1, groups):
                total = total + fars[n][lax.rem(chip - source + groups, groups), k].astype(F32)
            outs[n][part(side, k), :] = total.astype(outs[n].dtype)
            place = outs[n].at[part(side, k)]
            third[k, n] = remote(place, place, send_c.at[n, k], recv_c.at[n, k], sibling)
        for copy in list(first.values()) + list(second.values()):
            copy.wait_send()
        for copy in third.values():
            copy.wait()

    dma = pltpu.SemaphoreType.DMA
    whole = pl.BlockSpec(memory_space=pltpu.VMEM)
    return pl.pallas_call(
        body,
        in_specs=[whole] * count,
        out_specs=[whole] * count,
        out_shape=[jax.ShapeDtypeStruct(x.shape, x.dtype) for x in arrays],
        scratch_shapes=[pltpu.VMEM((PIECES, rows, x.shape[1]), x.dtype) for x in arrays]
        + [pltpu.VMEM((groups, PIECES, rows, x.shape[1]), x.dtype) for x in arrays]
        + [
            dma((count, PIECES)), dma((count, PIECES)), dma((count, groups, PIECES)),
            dma((count, groups, PIECES)), dma((count, PIECES)), dma((count, PIECES)),
        ],
        compiler_params=pltpu.CompilerParams(
            collective_id=collective_id, has_side_effects=True, vmem_limit_bytes=40 * 1024 * 1024
        ),
        cost_estimate=cost(micros),
        name="wide_sum",
    )(*arrays)


def cost(micros):
    return pl.CostEstimate(
        flops=int(micros * 1e9), bytes_accessed=int(micros * 3.6e6), transcendentals=0
    )


def call(body, blocks, ins, outs, scratch, backward, name, micros):
    def spec(shape, kind):
        if kind == "whole":
            return pl.BlockSpec(shape, lambda i: (0,) * len(shape))
        if kind == "lanes":
            block = (shape[0], shape[1] // blocks)
            return pl.BlockSpec(block, (lambda i: (0, blocks - 1 - i)) if backward else (lambda i: (0, i)))
        block = (shape[0] // blocks, shape[1])
        return pl.BlockSpec(block, (lambda i: (blocks - 1 - i, 0)) if backward else (lambda i: (i, 0)))

    return pl.pallas_call(
        body,
        grid=(blocks,),
        in_specs=[spec(a.shape, kind) for a, kind in ins],
        out_specs=[spec(shape, kind) for shape, _, kind in outs],
        out_shape=[jax.ShapeDtypeStruct(shape, dtype) for shape, dtype, _ in outs],
        scratch_shapes=scratch,
        compiler_params=pltpu.CompilerParams(
            dimension_semantics=("arbitrary",), vmem_limit_bytes=60 * 1024 * 1024
        ),
        cost_estimate=cost(micros),
        name=name,
    )(*[a for a, _ in ins])


def pad_rows(parts, width):
    rows = [jnp.pad(p.astype(F32), ((0, 0), (0, width - p.shape[1]))) for p in parts]
    used = sum(r.shape[0] for r in rows)
    return jnp.concatenate(rows + [jnp.zeros((8 - used, width), F32)], axis=0)


def per_device(
    tokens, cotangent, segments, norm_gain, gate_proj, value_proj, shared_proj, step_proj,
    conv_value, bias_value, conv_shared, bias_shared, step_bias, decay_log, skip_gain,
    gate_gain, out_proj,
):
    tp_count = lax.axis_size("tensor")
    length, width = tokens.shape
    inner = gate_proj.shape[1]
    heads = step_proj.shape[1]
    shared_width = shared_proj.shape[1]
    state_size = shared_width // 2
    blocks = length // SPAN
    aux, segr = pl.pallas_call(
        prep_kernel,
        out_shape=[
            jax.ShapeDtypeStruct((length, LANES), F32),
            jax.ShapeDtypeStruct((1, length), F32),
        ],
        name="prep_step",
    )(segments)
    ng = norm_gain[None, :]
    wst = jnp.pad(step_proj, ((0, 0), (0, LANES - heads)))
    chp = pad_rows(
        [conv_value, bias_value[None], gate_gain[None], jnp.repeat(skip_gain, HSIZE)[None]], inner
    )
    shp = pad_rows([conv_shared, bias_shared[None]], shared_width)
    hp = pad_rows([step_bias[None], -jnp.exp(decay_log)[None]], LANES)

    (
        hidden, gate_pre, value_pre, conv_out, shared_pre, shared_conv, z, ld, ldt, yn, sin, gn, stat,
    ) = call(
        fwd_kernel,
        blocks,
        [
            (tokens, "rows"), (cotangent, "rows"), (aux, "rows"), (segr, "lanes"), (ng, "whole"),
            (gate_proj, "whole"), (value_proj, "whole"), (shared_proj, "whole"), (wst, "whole"),
            (out_proj, "whole"), (chp, "whole"), (shp, "whole"), (hp, "whole"),
        ],
        [
            ((length, width), BF16, "rows"),
            ((length, inner), F32, "rows"),
            ((length, inner), F32, "rows"),
            ((length, inner), F32, "rows"),
            ((length, shared_width), F32, "rows"),
            ((length, shared_width), F32, "rows"),
            ((length, LANES), F32, "rows"),
            ((length, LANES), F32, "rows"),
            ((8, length), F32, "lanes"),
            ((length, inner), F32, "rows"),
            ((blocks * state_size, inner), F32, "rows"),
            ((length, inner), F32, "rows"),
            ((8, length), F32, "lanes"),
        ],
        [
            pltpu.VMEM((SPAN + 8, inner), F32),
            pltpu.VMEM((SPAN + 8, shared_width), F32),
            pltpu.VMEM((state_size, inner), F32),
        ],
        False,
        "fwd_scan",
        20,
    )
    stat = small_sum(stat, "tensor", 0)
    total_inner = float(inner * tp_count)

    def gate_body(*refs):
        gate_kernel(total_inner, *refs)

    normal_out, dy, gate_low, gain_part, mixed_part = call(
        gate_body,
        blocks,
        [
            (gate_pre, "rows"), (conv_out, "rows"), (yn, "rows"), (gn, "rows"), (stat, "lanes"),
            (chp, "whole"), (out_proj, "whole"),
        ],
        [
            ((length, inner), BF16, "rows"),
            ((length, inner), F32, "rows"),
            ((length, inner), BF16, "rows"),
            ((8, inner), F32, "whole"),
            ((length, width), BF16, "rows"),
        ],
        [],
        False,
        "gate_step",
        9,
    )
    mixed = lax.psum(mixed_part, "tensor")
    value_low, step_low, heads_part, dbc_part, ch_grads, head_grads = call(
        bwd_kernel,
        blocks,
        [
            (dy, "rows"), (conv_out, "rows"), (value_pre, "rows"), (shared_conv, "rows"),
            (z, "rows"), (ld, "rows"), (ldt, "lanes"), (yn, "rows"), (sin, "rows"),
            (aux, "rows"), (segr, "lanes"), (gate_low, "rows"), (gate_proj, "whole"),
            (value_proj, "whole"), (wst, "whole"), (chp, "whole"), (hp, "whole"),
        ],
        [
            ((length, inner), BF16, "rows"),
            ((length, LANES), BF16, "rows"),
            ((length, width), BF16, "rows"),
            ((length, shared_width), F32, "rows"),
            ((8, inner), F32, "whole"),
            ((8, LANES), F32, "whole"),
        ],
        [pltpu.VMEM((SPAN + 8, inner), F32), pltpu.VMEM((state_size, inner), F32)],
        True,
        "bwd_scan",
        27,
    )
    early_part = (
        jnp.concatenate(
            [
                t_mm(hidden, jnp.concatenate([gate_low, value_low, step_low], axis=1)),
                t_mm(cotangent, normal_out),
            ],
            axis=1,
        ).astype(BF16)
    )
    early_part, heads_part, mixed = lax.optimization_barrier((early_part, heads_part, mixed))
    early_part, mixed = lax.optimization_barrier((early_part, mixed))
    early = lax.psum_scatter(early_part, "dp", scatter_dimension=0, tiled=True).astype(F32)
    heads_sum, dbc = wide_sum((heads_part, dbc_part), "tensor", 1, 30)
    grad_tokens, shared_low, sh_grads, norm_part = call(
        end_kernel,
        blocks,
        [
            (heads_sum, "rows"), (dbc, "rows"), (shared_conv, "rows"), (shared_pre, "rows"), (aux, "rows"),
            (tokens, "rows"), (cotangent, "rows"),
            (ng, "whole"), (shared_proj, "whole"), (shp, "whole"),
        ],
        [
            ((length, width), BF16, "rows"),
            ((length, shared_width), BF16, "rows"),
            ((8, shared_width), F32, "whole"),
            ((8, width), F32, "whole"),
        ],
        [pltpu.VMEM((SPAN + 8, shared_width), F32)],
        True,
        "end_step",
        9,
    )
    shared_dots, early = lax.optimization_barrier((t_mm(hidden, shared_low).astype(BF16), early))
    late = lax.psum_scatter(
        shared_dots,
        "dp",
        scatter_dimension=0,
        tiled=True,
    ).astype(F32)
    col_width = width // tp_count
    norm_mine = lax.dynamic_slice_in_dim(
        norm_part[0], lax.axis_index("tensor") * col_width, col_width, 0
    )
    packed = jnp.concatenate(
        [
            norm_mine, ch_grads[:5].reshape(-1), sh_grads[:5].reshape(-1),
            head_grads[:3].reshape(-1), gain_part[0],
        ]
    )
    packed = packed.reshape(-1, LANES)
    packed = jnp.pad(packed, ((0, -packed.shape[0] % 8), (0, 0)))
    packed = small_sum(packed, "dp", 2).reshape(-1)
    sizes = [col_width, 5 * inner, 5 * shared_width, 3 * LANES, inner]
    pieces, start = [], 0
    for size in sizes:
        pieces.append(packed[start : start + size])
        start += size
    channel = pieces[1].reshape(5, inner)
    shared = pieces[2].reshape(5, shared_width)
    per_head = pieces[3].reshape(3, LANES)[:, :heads]
    result = (tokens.astype(F32) + mixed.astype(F32)).astype(BF16)
    return (
        result,
        grad_tokens,
        pieces[0],
        early[:, :inner],
        early[:, inner : 2 * inner],
        late,
        early[:, 2 * inner : 2 * inner + heads],
        channel[:4],
        channel[4],
        shared[:4],
        shared[4],
        per_head[0],
        per_head[1],
        per_head[2],
        pieces[4],
        early[:, 2 * inner + LANES :],
    )


def solution(mesh):
    rows, cols, vec = P("dp", None), P(None, "tensor"), P("tensor")
    return jax.shard_map(
        per_device,
        mesh=mesh,
        in_specs=(
            rows, rows, rows, P(), cols, cols, P(), cols, cols, vec, P(), P(), vec, vec, vec, vec, cols,
        ),
        out_specs=(
            rows, rows, vec, P("dp", "tensor"), P("dp", "tensor"), rows, P("dp", "tensor"), cols, vec,
            P(), P(), vec, vec, vec, vec, P("dp", "tensor"),
        ),
        check_vma=False,
    )
```
